256 devices in a mesh: rows: 8 (over y, core), cols: 32 (over x, z).
Axes of the slice: x: 4, y: 4, z: 8, core: 2. Of those that a mesh axis runs over, the one named last changes fastest.
Arguments:
- logged: bfloat16 [32768, 128], P(('rows', 'cols')), may hold values from -5 to 5
- targets: bfloat16 [65536, 128], P('cols'), may hold values from -5 to 5
- log_a: float32 [32768], P('rows'), may hold values from -2 to 2
- log_b: float32 [65536], P('cols'), may hold values from -2 to 2
- start_g: float32 [65536], P('cols'), may hold values from -2 to 142
Outputs:
- pot_f: float32 [32768], P('rows')
- pot_g: float32 [65536], P('cols')
The draws below stay inside these ranges and needn't reach their ends.
All inputs are finite; a program needn't handle non-finite values.
Results may differ from the reference program's by a relative error of at most 0.0003.
Values may be sent and summed in bfloat16 or wider, within the bound.
A program may use at most 64 MiB of HBM per device.

```python
import math
import jax
import jax.numpy as jnp
from jax import lax

W = 128
ITERS = 3
N = 32768
M = 65536


def draw_start_g(key, part):
    base_key = jax.random.fold_in(key, 11)
    values = jnp.clip(jax.random.normal(base_key, (M,), jnp.float32) * 0.5, -2.0, 2.0)
    return values.astype(jnp.float32)


def block_levels(stream_key, dims, pieces, smallest, largest):
    level = 1.0
    for dim, blocks in pieces:
        steps = jax.random.uniform(jax.random.fold_in(jax.random.fold_in(stream_key, 6), dim), (blocks,), jnp.float32, smallest / len(pieces), largest / len(pieces))
        level = level * jnp.repeat(jnp.exp(steps), dims[dim] // blocks).reshape((-1,) + (1,) * (len(dims) - 1 - dim))
    return level


def normal_values(own_key, shape, spread, limit, split=(), held_as=jnp.bfloat16):
    array = spread * jax.random.normal(own_key, shape, jnp.float32)
    if split:
        array = array * block_levels(own_key, shape, split, -0.22, 0.18)
    return jnp.clip(array, -limit, limit).astype(held_as)


def setup_inputs(seed: int = 0) -> dict:
    streams_of = jax.random.split(jax.random.key(seed), 6)
    logged = normal_values(streams_of[0], (N, W), 1.25, 5.0, ((0, 256),))
    targets = normal_values(streams_of[1], (M, W), 1.25, 5.0, ((0, 32),))
    log_a = jnp.clip(jax.random.uniform(streams_of[2], (N,), jnp.float32, -2.0, 2.0) * block_levels(streams_of[2], (N,), ((0, 8),), -0.4, 0.0), -2.0, 2.0)
    log_b = jnp.clip(jax.random.uniform(streams_of[3], (M,), jnp.float32, -2.0, 2.0) * block_levels(streams_of[3], (M,), ((0, 32),), -0.4, 0.0), -2.0, 2.0)
    start_g = draw_start_g(jax.random.fold_in(streams_of[5], 71), 0)
    return {"logged": logged, "targets": targets, "log_a": log_a, "log_b": log_b, "start_g": start_g}


EPS = 0.5


def row_pass(logged, targets, lx, ly, log_b, pot_g):
    block = math.gcd(N, 1024)

    def one(item):
        xb, xn = item
        inner = jnp.dot(xb, targets.T, preferred_element_type=jnp.float32)
        cost = xn[:, None] + ly[None, :] - 2.0 * inner
        s = log_b[None, :] + (pot_g[None, :] - cost) / EPS
        top = jnp.max(s, axis=1)
        total = jnp.sum(jnp.exp(s - top[:, None]), axis=1)
        return -EPS * (top + jnp.log(total))

    out = lax.map(one, (logged.reshape(N // block, block, W), lx.reshape(N // block, block)))
    return out.reshape(N)


def col_pass(logged, targets, lx, ly, log_a, pot_f):
    block = math.gcd(M, 1024)

    def one(item):
        yb, yn = item
        inner = jnp.dot(logged, yb.T, preferred_element_type=jnp.float32)
        cost = lx[:, None] + yn[None, :] - 2.0 * inner
        s = log_a[:, None] + (pot_f[:, None] - cost) / EPS
        top = jnp.max(s, axis=0)
        total = jnp.sum(jnp.exp(s - top[None, :]), axis=0)
        return -EPS * (top + jnp.log(total))

    out = lax.map(one, (targets.reshape(M // block, block, W), ly.reshape(M // block, block)))
    return out.reshape(M)


def reference(logged, targets, log_a, log_b, start_g):
    lx = jnp.sum(jnp.square(logged.astype(jnp.float32)), axis=1)
    ly = jnp.sum(jnp.square(targets.astype(jnp.float32)), axis=1)
    pot_g = start_g
    pot_f = jnp.zeros((N,), jnp.float32)
    for step in range(ITERS):
        pot_f = row_pass(logged, targets, lx, ly, log_b, pot_g)
        pot_g = col_pass(logged, targets, lx, ly, log_a, pot_f)
    return pot_f, pot_g
```

```python
import functools

import jax
import jax.numpy as jnp
from jax import lax
from jax.experimental import pallas as pl
from jax.experimental.pallas import tpu as pltpu
from jax.sharding import PartitionSpec as P

NX, NZ, NR = 4, 8, 8
F32, BF16 = jnp.float32, jnp.bfloat16
NT = (((1,), (1,)), ((), ()))
TI = 256
TJ = 256
MESH = pl.DeviceIdType.MESH


def dot(a, b, dims=(((1,), (0,)), ((), ()))):
    return lax.dot_general(a, b, dims, preferred_element_type=F32)


def flat(ref, rows, start=0):
    return jnp.concatenate([ref[start + k : start + k + 1, :] for k in range(rows)], axis=1)


def put(ref, value, start=0):
    for k in range(value.shape[1] // 128):
        ref[start + k : start + k + 1, :] = value[:, k * 128 : (k + 1) * 128]


def pieces(value, count):
    out = []
    for k in range(count):
        part = value.astype(BF16).astype(F32)
        out.append(part)
        value = value - part
    return out


def stack_pieces(value, count, rows=16):
    n = value.shape[1]
    index = lax.broadcasted_iota(jnp.int32, (rows, n), 0)
    out = jnp.zeros((rows, n), F32)
    for k, part in enumerate(pieces(value, count)):
        out = jnp.where(index == k, jnp.broadcast_to(part, (rows, n)), out)
    return out.astype(BF16)


def selector(rows, count):
    return (lax.broadcasted_iota(jnp.int32, (rows, 128), 1) < count).astype(F32).astype(BF16)


def square_sums(block):
    wide = block.astype(F32)
    high, low = pieces(wide * wide, 2)
    ones = jnp.ones((8, block.shape[1]), BF16)
    total = dot(ones, high.astype(BF16), NT) + dot(ones, low.astype(BF16), NT)
    return total[0:1, :]


def columns_of(stacked, eye):
    return dot(eye, stacked, NT).astype(BF16)


def kernel(
    x_ref, y_ref, la_ref, lb_ref, g_ref, f_out, g_out,
    xv, ya, p, eye, sel, mt, ct, w, alpha, beta, rowstat, colstat, xn, yn, v1, lse,
    xbuf, zbuf, rbuf,
    gx_send, gx_recv, gz_send, gz_recv, x_send, x_recv, z_send, z_recv, r_send, r_recv,
):
    n, m = xv.shape[0], ya.shape[0]
    nb, mb = n // 128, m // 128
    tiles = n // TI
    row = lax.axis_index("rows")
    col = lax.axis_index("cols")
    px, pz = col // NZ, lax.rem(col, NZ)

    def at_x(k):
        return (row, lax.rem(px + k, NX) * NZ + pz)

    def at_z(k):
        return (row, px * NZ + lax.rem(pz + k, NZ))

    def at_r(k):
        return (lax.rem(row + k, NR), col)

    barrier = pltpu.get_barrier_semaphore()
    for at, count in ((at_x, NX), (at_z, NZ), (at_r, NR)):
        for k in range(1, count):
            pl.semaphore_signal(barrier, inc=1, device_id=at(k), device_id_type=MESH)
    pl.semaphore_wait(barrier, NX + NZ + NR - 3)

    def shard(cx, cz):
        return xv.at[pl.ds(pl.multiple_of((cx * NZ + cz) * 128, 128), 128), pl.ds(0, 128)]

    def remote(src, dst, send, recv, device):
        return pltpu.make_async_remote_copy(
            src_ref=src, dst_ref=dst, send_sem=send, recv_sem=recv, device_id=device, device_id_type=MESH
        )

    def x_copy(k):
        own = shard(px, pz)
        return remote(own, own, gx_send.at[k], gx_recv.at[k], at_x(k))

    def z_copy(cx, cz, way, slot):
        block = shard(cx, cz)
        return remote(block, block, gz_send.at[way, slot], gz_recv.at[way, slot], at_z(1 if way == 0 else NZ - 1))

    def came_x(s):
        return lax.rem(px + NX - s, NX)

    own_rows = pl.ds(pl.multiple_of(col * 128, 128), 128)
    xv[own_rows, 0:128] = x_ref[...]
    for k in range(1, NX):
        x_copy(k).start()
    for way in range(2):
        z_copy(px, pz, way, 0).start()

    index = lax.broadcasted_iota(jnp.int32, (TI, TI), 0) == lax.broadcasted_iota(jnp.int32, (TI, TI), 1)
    eye[...] = jnp.where(index, 1.0, 0.0).astype(BF16)
    sel[...] = selector(TI, 3)
    ya[:, 128:256] = jnp.zeros((m, 128), BF16)
    xv[:, 128:256] = jnp.zeros((n, 128), BF16)
    for k in range(m // TI):
        cut = pl.ds(k * TI, TI)
        block = y_ref[cut, :]
        ya[cut, 0:128] = (block.astype(F32) * 4.0).astype(BF16)
        norm = square_sums(block)
        put(yn, norm, 2 * k)
        u = lb_ref[:, cut] + 2.0 * g_ref[:, cut] - 2.0 * norm
        ya[cut, 128:144] = columns_of(stack_pieces(u, 3), eye[...])

    for s in range(1, NX):
        x_copy(s).wait_recv()
        for way in range(2):
            z_copy(came_x(s), pz, way, s).start()

    def pair(first, second):
        rows_1 = pl.ds(pl.multiple_of(first * 128, 128), 128)
        rows_2 = pl.ds(pl.multiple_of(second * 128, 128), 128)
        points = jnp.concatenate([xv[rows_1, 0:128], xv[rows_2, 0:128]], axis=0)
        points = jnp.concatenate([points, sel[...]], axis=1)
        top = total = None
        for k in range(m // TJ):
            s = dot(ya[k * TJ : (k + 1) * TJ, :], points, NT).reshape(TJ // 8, 8, 256)
            here = jnp.max(s, axis=0)
            if k == 0:
                top = here
                total = jnp.sum(jnp.exp(s - top[None]), axis=0)
            else:
                upper = jnp.maximum(top, here)
                total = total * jnp.exp(top - upper) + jnp.sum(jnp.exp(s - upper[None]), axis=0)
                top = upper
        best = jnp.max(top, axis=0, keepdims=True)
        whole = jnp.sum(total * jnp.exp(top - best), axis=0, keepdims=True)
        for ref, value in ((0, best), (nb, whole)):
            rowstat[pl.ds(ref + first, 1), :] = value[:, 0:128]
            rowstat[pl.ds(ref + second, 1), :] = value[:, 128:256]

    def near(k, carry):
        pair(came_x(2 * k) * NZ + pz, came_x(2 * k + 1) * NZ + pz)
        return carry

    def middle(k, carry):
        hop, s = k // NX + 1, lax.rem(k, NX)
        cx = came_x(s)
        up, down = lax.rem(pz + NZ - hop, NZ), lax.rem(pz + hop, NZ)
        z_copy(cx, up, 0, k).wait_recv()
        z_copy(cx, down, 1, k).wait_recv()

        @pl.when((k < 2 * NX) | ((k >= 2 * NX) & (s < 2)))
        def forward_up():
            z_copy(cx, up, 0, k + NX).start()

        @pl.when(k < 2 * NX)
        def forward_down():
            z_copy(cx, down, 1, k + NX).start()

        @pl.when((k >= 2 * NX) & (s >= 2))
        def forward_last():
            z_copy(cx, down, 1, k + NX - 2).start()

        pair(cx * NZ + up, cx * NZ + down)
        return carry

    def far(k, carry):
        opposite = lax.rem(pz + NZ // 2, NZ)

        @pl.when(k == 0)
        def from_up():
            for s in range(2):
                z_copy(came_x(s), opposite, 0, 3 * NX + s).wait_recv()

        @pl.when(k == 1)
        def from_down():
            for s in range(2):
                z_copy(came_x(s + 2), opposite, 1, 3 * NX + s).wait_recv()

        pair(came_x(2 * k) * NZ + opposite, came_x(2 * k + 1) * NZ + opposite)
        return carry

    lax.fori_loop(0, 2, near, 0)
    lax.fori_loop(0, 3 * NX, middle, 0)
    lax.fori_loop(0, 2, far, 0)

    def spread(buf, send, recv, at, me, count, rows):
        view = pl.ds(0, rows)
        for k in range(1, count):
            own = buf.at[me, view, :]
            remote(own, own, send.at[k], recv.at[k], at(k)).start()

    def collect(buf, send, recv, at, me, count, rows):
        view = pl.ds(0, rows)
        for k in range(1, count):
            own = buf.at[me, view, :]
            remote(own, own, send.at[k], recv.at[k], at(k)).wait()

    def join(buf, count, size):
        tops = [buf[k, 0:size, :] for k in range(count)]
        sums = [buf[k, size : 2 * size, :] for k in range(count)]
        top = functools.reduce(jnp.maximum, tops)
        total = functools.reduce(lambda a, b: a + b, [s * jnp.exp(t - top) for t, s in zip(tops, sums)])
        return top, total

    def add(buf, count, size):
        return functools.reduce(lambda a, b: a + b, [buf[k, 0:size, :] for k in range(count)])

    def over(buf, send, recv, at, me, count, rows, meanwhile=None):
        spread(buf, send, recv, at, me, count, rows)
        if meanwhile is not None:
            meanwhile()
        collect(buf, send, recv, at, me, count, rows)

    def over_x(step, rows, meanwhile=None):
        over(xbuf.at[step], x_send.at[step], x_recv.at[step], at_x, px, NX, rows, meanwhile)

    def over_z(step, rows):
        over(zbuf.at[step], z_send.at[step], z_recv.at[step], at_z, pz, NZ, rows)

    def over_r(step, rows):
        over(rbuf.at[step], r_send.at[step], r_recv.at[step], at_r, row, NR, rows)

    def row_norms():
        def one(k, carry):
            norm = square_sums(xv[pl.ds(pl.multiple_of(k * TI, TI), TI), 0:128])
            xn[pl.ds(2 * k, 1), :] = norm[:, 0:128]
            xn[pl.ds(2 * k + 1, 1), :] = norm[:, 128:256]
            return carry

        lax.fori_loop(0, tiles, one, 0)

    xbuf[0, px] = rowstat[...]
    over_x(0, 2 * nb, row_norms)
    top, total = join(xbuf.at[0], NX, nb)
    zbuf[0, pz, 0:nb, :] = top
    zbuf[0, pz, nb : 2 * nb, :] = total
    over_z(0, 2 * nb)
    top, total = join(zbuf.at[0], NZ, nb)
    v1[...] = la_ref[...] - (top + jnp.log(total))
    alpha[...] = stack_pieces(flat(v1, nb), 3)

    def place(k, carry):
        cut = pl.ds(pl.multiple_of(k * TI, TI), TI)
        xv[cut, 128:144] = columns_of(alpha[:, cut], eye[...])
        return carry

    lax.fori_loop(0, tiles, place, 0)

    def tile(t, carry):
        cut = pl.ds(pl.multiple_of(t * TI, TI), TI)
        points = xv[cut, :]
        for k in range(m // 256):
            lanes = slice(k * 256, (k + 1) * 256)
            weights = jnp.concatenate([ya[lanes, 0:128], sel[...]], axis=1)
            s = dot(points, weights, NT)
            top = jnp.max(s, axis=0, keepdims=True)
            e = jnp.exp(s - top)
            mt[pl.ds(t, 1), lanes] = top
            ct[pl.ds(t, 1), lanes] = jnp.sum(e, axis=0, keepdims=True)
            p[cut, lanes] = e.astype(BF16)
        return carry

    lax.fori_loop(0, tiles, tile, 0)
    top = jnp.max(mt[...], axis=0, keepdims=True)
    total = jnp.sum(ct[...] * jnp.exp(mt[...] - top), axis=0, keepdims=True)
    put(rbuf.at[0, row], top)
    put(rbuf.at[0, row], total, mb)
    over_r(0, 2 * mb)
    top, total = join(rbuf.at[0], NR, mb)
    lse[...] = top + jnp.log(total)
    w[...] = jnp.exp(mt[...] - flat(lse, mb))
    weight_b = jnp.exp(lb_ref[...])

    def row_product(step, scale):
        full = w[...] * scale
        high = full.astype(BF16)
        beta[0:tiles, :] = high
        beta[tiles : 2 * tiles, :] = (full - high.astype(F32)).astype(BF16)

        def one(t, carry):
            cut = pl.ds(pl.multiple_of(t * TI, TI), TI)
            out = dot(beta[...], p[cut, :], NT)
            which = lax.broadcasted_iota(jnp.int32, out.shape, 0)
            mine = jnp.sum(jnp.where((which == t) | (which == t + tiles), out, 0.0), axis=0, keepdims=True)
            xbuf[step, px, pl.ds(2 * t, 1), :] = mine[:, 0:128]
            xbuf[step, px, pl.ds(2 * t + 1, 1), :] = mine[:, 128:256]
            return carry

        lax.fori_loop(0, tiles, one, 0)
        over_x(step, nb)
        zbuf[step, pz, 0:nb, :] = add(xbuf.at[step], NX, nb)
        over_z(step, nb)
        return add(zbuf.at[step], NZ, nb)

    def col_product(step, rowsum):
        rowstat[0:nb, :] = jnp.exp(la_ref[...]) / rowsum
        alpha[...] = stack_pieces(flat(rowstat, nb), 2)

        def one(t, acc):
            cut = pl.ds(pl.multiple_of(t * TI, TI), TI)
            out = dot(alpha[:, cut], p[cut, :])
            return acc + out[0:8, :] * w[pl.ds(t, 1), :]

        acc = lax.fori_loop(0, tiles, one, jnp.zeros((8, m), F32))
        put(rbuf.at[step, row], jnp.sum(acc, axis=0, keepdims=True))
        over_r(step, mb)
        return add(rbuf.at[step], NR, mb)

    rowsum = row_product(1, weight_b)
    colsum = col_product(1, rowsum)
    colstat[...] = colsum
    rowsum = row_product(2, weight_b / flat(colstat, mb))
    f_out[...] = xn[...] + 0.5 * (v1[...] - jnp.log(rowsum))
    colsum = col_product(2, rowsum)
    g_out[...] = yn[...] - 0.5 * (lse[...] + jnp.log(colsum))

    for k in range(1, NX):
        x_copy(k).wait_send()
    for slot in range(3 * NX + 2):
        for way in range(2):
            z_copy(px, pz, way, slot).wait_send()


def local(logged, targets, log_a, log_b, start_g):
    n, m = log_a.shape[0], log_b.shape[0]
    nb, mb = n // 128, m // 128
    tiles = n // TI
    dma = pltpu.SemaphoreType.DMA
    vmem = pl.BlockSpec(memory_space=pltpu.VMEM)
    f, g = pl.pallas_call(
        kernel,
        out_shape=(jax.ShapeDtypeStruct((nb, 128), F32), jax.ShapeDtypeStruct((mb, 128), F32)),
        in_specs=[vmem] * 5,
        out_specs=(vmem, vmem),
        scratch_shapes=[
            pltpu.VMEM((n, 256), BF16),
            pltpu.VMEM((m, 256), BF16),
            pltpu.VMEM((n, m), BF16),
            pltpu.VMEM((TI, TI), BF16),
            pltpu.VMEM((TI, 128), BF16),
            pltpu.VMEM((tiles, m), F32),
            pltpu.VMEM((tiles, m), F32),
            pltpu.VMEM((tiles, m), F32),
            pltpu.VMEM((16, n), BF16),
            pltpu.VMEM((2 * tiles, m), BF16),
            pltpu.VMEM((2 * nb, 128), F32),
            pltpu.VMEM((mb, 128), F32),
            pltpu.VMEM((nb, 128), F32),
            pltpu.VMEM((mb, 128), F32),
            pltpu.VMEM((nb, 128), F32),
            pltpu.VMEM((mb, 128), F32),
            pltpu.VMEM((3, NX, 2 * nb, 128), F32),
            pltpu.VMEM((3, NZ, 2 * nb, 128), F32),
            pltpu.VMEM((3, NR, 2 * mb, 128), F32),
            dma((NX,)),
            dma((NX,)),
            dma((2, 3 * NX + 2)),
            dma((2, 3 * NX + 2)),
            dma((3, NX)),
            dma((3, NX)),
            dma((3, NZ)),
            dma((3, NZ)),
            dma((3, NR)),
            dma((3, NR)),
        ],
        compiler_params=pltpu.CompilerParams(
            collective_id=0, has_side_effects=True, vmem_limit_bytes=50 * 1024 * 1024
        ),
    )(logged, targets, log_a.reshape(nb, 128), log_b.reshape(1, m), start_g.reshape(1, m))
    return f.reshape(n), g.reshape(m)


def solution(mesh):
    placed = (P(("rows", "cols"), None), P("cols", None), P("rows"), P("cols"), P("cols"))
    return jax.shard_map(
        local, mesh=mesh, in_specs=placed, out_specs=(P("rows"), P("cols")), check_vma=False
    )
```

```python
import functools

import jax
import jax.numpy as jnp
from jax import lax
from jax.experimental import pallas as pl
from jax.experimental.pallas import tpu as pltpu
from jax.sharding import PartitionSpec as P

NX, NZ, NR = 4, 8, 8
F32, BF16 = jnp.float32, jnp.bfloat16
NT = (((1,), (1,)), ((), ()))
TI = 256
TJ = 256
WIDE = 1024
MESH = pl.DeviceIdType.MESH


def dot(a, b, dims=(((1,), (0,)), ((), ()))):
    return lax.dot_general(a, b, dims, preferred_element_type=F32)


def flat(ref, rows, start=0):
    return jnp.concatenate([ref[start + k : start + k + 1, :] for k in range(rows)], axis=1)


def put(ref, value, start=0):
    for k in range(value.shape[1] // 128):
        ref[start + k : start + k + 1, :] = value[:, k * 128 : (k + 1) * 128]


def pieces(value, count):
    out = []
    for k in range(count):
        part = value.astype(BF16).astype(F32)
        out.append(part)
        value = value - part
    return out


def stack_pieces(value, count, rows=16):
    n = value.shape[1]
    index = lax.broadcasted_iota(jnp.int32, (rows, n), 0)
    out = jnp.zeros((rows, n), F32)
    for k, part in enumerate(pieces(value, count)):
        out = jnp.where(index == k, jnp.broadcast_to(part, (rows, n)), out)
    return out.astype(BF16)


def selector(rows, count):
    return (lax.broadcasted_iota(jnp.int32, (rows, 128), 1) < count).astype(F32).astype(BF16)


def square_sums(block):
    wide = block.astype(F32)
    high, low = pieces(wide * wide, 2)
    ones = jnp.ones((8, block.shape[1]), BF16)
    total = dot(ones, high.astype(BF16), NT) + dot(ones, low.astype(BF16), NT)
    return total[0:1, :]


def columns_of(stacked, eye):
    return dot(eye, stacked, NT).astype(BF16)


def kernel(
    x_hbm, y_hbm, la_hbm, lb_hbm, g_hbm, f_out, g_out,
    y_ref, la_ref, lb_ref, g_ref,
    xv, ya, p, eye, sel, mt, ct, w, alpha, beta, rowstat, colstat, xn, yn, v1, lse,
    xpair, zpair, rpair, xbuf, zbuf, rbuf, local_sem,
    gx_send, gx_recv, gz_send, gz_recv, x_send, x_recv, z_send, z_recv, r_send, r_recv,
):
    n, m = xv.shape[0], ya.shape[0]
    nb, mb = n // 128, m // 128
    tiles = n // TI
    row = lax.axis_index("rows")
    col = lax.axis_index("cols")
    px, pz = col // NZ, lax.rem(col, NZ)

    def at_x(k):
        return (row, lax.rem(px + k, NX) * NZ + pz)

    def at_z(k):
        return (row, px * NZ + lax.rem(pz + k, NZ))

    def at_r(k):
        return (lax.rem(row + k, NR), col)

    barrier = pltpu.get_barrier_semaphore()
    for at, count in ((at_x, NX), (at_z, NZ), (at_r, NR)):
        for k in range(1, count):
            pl.semaphore_signal(barrier, inc=1, device_id=at(k), device_id_type=MESH)

    own_rows = pl.ds(pl.multiple_of(col * 128, 128), 128)
    moves = (
        (x_hbm, xv.at[own_rows, pl.ds(0, 128)]), (y_hbm, y_ref), (la_hbm, la_ref), (lb_hbm, lb_ref), (g_hbm, g_ref),
    )
    fetch = [pltpu.make_async_copy(src, dst, local_sem.at[k]) for k, (src, dst) in enumerate(moves)]
    for one in fetch:
        one.start()
    index = lax.broadcasted_iota(jnp.int32, (TI, TI), 0) == lax.broadcasted_iota(jnp.int32, (TI, TI), 1)
    eye[...] = jnp.where(index, 1.0, 0.0).astype(BF16)
    sel[...] = selector(sel.shape[0], 3)
    ya[:, 128:256] = jnp.zeros((m, 128), BF16)
    xv[:, 128:256] = jnp.zeros((n, 128), BF16)
    fetch[0].wait()
    pl.semaphore_wait(barrier, NX + NZ + NR - 3)

    def remote(src, dst, send, recv, device):
        return pltpu.make_async_remote_copy(
            src_ref=src, dst_ref=dst, send_sem=send, recv_sem=recv, device_id=device, device_id_type=MESH
        )

    def came_x(s):
        return lax.rem(px + NX - s, NX)

    def came_z(k):
        return lax.rem(pz + NZ - k, NZ)

    def shard_rows(cx, cz):
        return pl.ds(pl.multiple_of((cx * NZ + cz) * 128, 128), 128)

    def shard(cx, cz):
        return xv.at[shard_rows(cx, cz), pl.ds(0, 128)]

    def z_copy(k):
        own = shard(px, pz)
        return remote(own, own, gz_send.at[k], gz_recv.at[k], at_z(k))

    def x_copy(k, s):
        block = shard(px, came_z(k))
        return remote(block, block, gx_send.at[k, s], gx_recv.at[k, s], at_x(s))

    def turn(q):
        odd = lax.rem(q, 2)
        return odd * ((q + 1) // 2) + (1 - odd) * lax.rem(NZ - q // 2, NZ)

    for s in range(1, NX):
        x_copy(0, s).start()
    for q in range(1, NZ):
        z_copy((q + 1) // 2 if q % 2 else NZ - q // 2).start()
    for one in fetch[1:]:
        one.wait()

    for k in range(m // TI):
        cut = pl.ds(k * TI, TI)
        block = y_ref[cut, :]
        ya[cut, 0:128] = (block.astype(F32) * 4.0).astype(BF16)
        norm = square_sums(block)
        put(yn, norm, 2 * k)
        u = lb_ref[:, cut] + 2.0 * g_ref[:, cut] - 2.0 * norm
        ya[cut, 128:144] = columns_of(stack_pieces(u, 3), eye[...])

    def forward(q):
        k = turn(q)
        z_copy(k).wait_recv()
        for s in range(1, NX):
            x_copy(k, s).start()

    def pass_1(q, carry):
        @pl.when(q < NZ - 2)
        def ahead():
            forward(q + 2)

        k = turn(q)
        for s in range(1, NX):
            remote(shard(came_x(s), came_z(k)), shard(came_x(s), came_z(k)), gx_send.at[k, s], gx_recv.at[k, s],
                   at_x(s)).wait_recv()
        points = jnp.concatenate([xv[shard_rows(came_x(s), came_z(k)), 0:128] for s in range(NX)], axis=0)
        points = jnp.concatenate([points, sel[0 : NX * 128, :]], axis=1)
        top = total = None
        for j in range(m // TJ):
            s = dot(ya[j * TJ : (j + 1) * TJ, :], points, NT).reshape(TJ // 8, 8, NX * 128)
            here = jnp.max(s, axis=0)
            if j == 0:
                top = here
                total = jnp.sum(jnp.exp(s - top[None]), axis=0)
            else:
                upper = jnp.maximum(top, here)
                total = total * jnp.exp(top - upper) + jnp.sum(jnp.exp(s - upper[None]), axis=0)
                top = upper
        best = jnp.max(top, axis=0, keepdims=True)
        whole = jnp.sum(total * jnp.exp(top - best), axis=0, keepdims=True)
        for start, value in ((0, best), (nb, whole)):
            for s in range(NX):
                rowstat[pl.ds(start + came_x(s) * NZ + came_z(k), 1), :] = value[:, s * 128 : (s + 1) * 128]
        return carry

    forward(1)
    lax.fori_loop(0, NZ, pass_1, 0)

    def spread(buf, send, recv, at, me, count, rows):
        view = pl.ds(0, rows)
        for k in range(1, count):
            own = buf.at[me, view, :]
            remote(own, own, send.at[k], recv.at[k], at(k)).start()

    def collect(buf, send, recv, at, me, count, rows):
        view = pl.ds(0, rows)
        for k in range(1, count):
            own = buf.at[me, view, :]
            remote(own, own, send.at[k], recv.at[k], at(k)).wait()

    def join(buf, count, size):
        tops = [buf[k, 0:size, :].astype(F32) for k in range(count)]
        sums = [buf[k, size : 2 * size, :].astype(F32) for k in range(count)]
        top = functools.reduce(jnp.maximum, tops)
        total = functools.reduce(lambda a, b: a + b, [s * jnp.exp(t - top) for t, s in zip(tops, sums)])
        return top, total

    def add(buf, count, size):
        return functools.reduce(lambda a, b: a + b, [buf[k, 0:size, :].astype(F32) for k in range(count)])

    def pack(ref, top, total):
        size = top.shape[0]
        near = top.astype(BF16)
        ref[0:size, :] = near
        ref[size : 2 * size, :] = (total * jnp.exp(top - near.astype(F32))).astype(BF16)

    def over(buf, send, recv, at, me, count, rows, meanwhile=None):
        spread(buf, send, recv, at, me, count, rows)
        if meanwhile is not None:
            meanwhile()
        collect(buf, send, recv, at, me, count, rows)

    def over_x(buf, step, meanwhile=None):
        over(buf, x_send.at[step], x_recv.at[step], at_x, px, NX, buf.shape[1], meanwhile)

    def over_z(buf, step):
        over(buf, z_send.at[step], z_recv.at[step], at_z, pz, NZ, buf.shape[1])

    def over_r(buf, step):
        over(buf, r_send.at[step], r_recv.at[step], at_r, row, NR, buf.shape[1])

    def row_norms():
        def one(k, carry):
            norm = square_sums(xv[pl.ds(pl.multiple_of(k * TI, TI), TI), 0:128])
            xn[pl.ds(2 * k, 1), :] = norm[:, 0:128]
            xn[pl.ds(2 * k + 1, 1), :] = norm[:, 128:256]
            return carry

        lax.fori_loop(0, tiles, one, 0)

    pack(xpair.at[px], rowstat[0:nb, :], rowstat[nb : 2 * nb, :])
    over_x(xpair, 0, row_norms)
    pack(zpair.at[pz], *join(xpair, NX, nb))
    over_z(zpair, 0)
    top, total = join(zpair, NZ, nb)
    v1[...] = la_ref[...] - (top + jnp.log(total))
    alpha[...] = stack_pieces(flat(v1, nb), 3)

    def place(k, carry):
        cut = pl.ds(pl.multiple_of(k * TI, TI), TI)
        xv[cut, 128:144] = columns_of(alpha[:, cut], eye[...])
        return carry

    lax.fori_loop(0, tiles, place, 0)

    def tile(t, carry):
        cut = pl.ds(pl.multiple_of(t * TI, TI), TI)
        points = xv[cut, :]
        for k in range(m // WIDE):
            lanes = slice(k * WIDE, (k + 1) * WIDE)
            weights = jnp.concatenate([ya[lanes, 0:128], sel[...]], axis=1)
            s = dot(points, weights, NT)
            top = jnp.max(s, axis=0, keepdims=True)
            e = jnp.exp(s - top)
            mt[pl.ds(t, 1), lanes] = top
            ct[pl.ds(t, 1), lanes] = jnp.sum(e, axis=0, keepdims=True)
            p[cut, lanes] = e.astype(BF16)
        return carry

    lax.fori_loop(0, tiles, tile, 0, unroll=2)
    top = jnp.max(mt[...], axis=0, keepdims=True)
    total = jnp.sum(ct[...] * jnp.exp(mt[...] - top), axis=0, keepdims=True)
    put(colstat, top)
    put(colstat, total, mb)
    pack(rpair.at[row], colstat[0:mb, :], colstat[mb : 2 * mb, :])
    over_r(rpair, 0)
    top, total = join(rpair, NR, mb)
    lse[...] = top + jnp.log(total)
    w[...] = jnp.exp(mt[...] - flat(lse, mb))
    weight_b = jnp.exp(lb_ref[...])

    def row_product(step, scale):
        full = w[...] * scale
        high = full.astype(BF16)
        beta[0:tiles, :] = high
        beta[tiles : 2 * tiles, :] = (full - high.astype(F32)).astype(BF16)

        for half in range(2):
            cut = pl.ds(half * (n // 2), n // 2)
            out = dot(beta[...], p[cut, :], NT)
            which = lax.broadcasted_iota(jnp.int32, out.shape, 0)
            own = lax.broadcasted_iota(jnp.int32, out.shape, 1) // TI + half * (tiles // 2)
            mine = jnp.sum(jnp.where((which == own) | (which == own + tiles), out, 0.0), axis=0, keepdims=True)
            put(rowstat, mine, half * (nb // 2))
        xbuf[step - 1, px] = rowstat[0:nb, :].astype(BF16)
        over_x(xbuf.at[step - 1], step)
        zbuf[step - 1, pz] = add(xbuf.at[step - 1], NX, nb).astype(BF16)
        over_z(zbuf.at[step - 1], step)
        return add(zbuf.at[step - 1], NZ, nb)

    def col_product(step, rowsum):
        rowstat[0:nb, :] = jnp.exp(la_ref[...]) / rowsum
        alpha[...] = stack_pieces(flat(rowstat, nb), 2)

        def one(t, acc):
            cut = pl.ds(pl.multiple_of(t * TI, TI), TI)
            out = dot(alpha[:, cut], p[cut, :])
            return acc + out[0:8, :] * w[pl.ds(t, 1), :]

        acc = lax.fori_loop(0, tiles, one, jnp.zeros((8, m), F32), unroll=16)
        put(rbuf.at[step - 1, row], jnp.sum(acc, axis=0, keepdims=True))
        over_r(rbuf.at[step - 1], step)
        return add(rbuf.at[step - 1], NR, mb)

    rowsum = row_product(1, weight_b)
    colsum = col_product(1, rowsum)
    colstat[0:mb, :] = colsum
    rowsum = row_product(2, weight_b / flat(colstat, mb))
    f_out[...] = xn[...] + 0.5 * (v1[...] - jnp.log(rowsum))
    colsum = col_product(2, rowsum)
    g_out[...] = yn[...] - 0.5 * (lse[...] + jnp.log(colsum))

    for k in range(NZ):
        if k:
            z_copy(k).wait_send()
        for s in range(1, NX):
            x_copy(k, s).wait_send()


def local(logged, targets, log_a, log_b, start_g):
    n, m = log_a.shape[0], log_b.shape[0]
    nb, mb = n // 128, m // 128
    tiles = n // TI
    dma = pltpu.SemaphoreType.DMA
    vmem = pl.BlockSpec(memory_space=pltpu.VMEM)
    anywhere = pl.BlockSpec(memory_space=pl.ANY)
    f, g = pl.pallas_call(
        kernel,
        out_shape=(jax.ShapeDtypeStruct((nb, 128), F32), jax.ShapeDtypeStruct((mb, 128), F32)),
        in_specs=[anywhere] * 5,
        out_specs=(vmem, vmem),
        scratch_shapes=[
            pltpu.VMEM((m, 128), BF16),
            pltpu.VMEM((nb, 128), F32),
            pltpu.VMEM((1, m), F32),
            pltpu.VMEM((1, m), F32),
            pltpu.VMEM((n, 256), BF16),
            pltpu.VMEM((m, 256), BF16),
            pltpu.VMEM((n, m), BF16),
            pltpu.VMEM((TI, TI), BF16),
            pltpu.VMEM((WIDE, 128), BF16),
            pltpu.VMEM((tiles, m), F32),
            pltpu.VMEM((tiles, m), F32),
            pltpu.VMEM((tiles, m), F32),
            pltpu.VMEM((16, n), BF16),
            pltpu.VMEM((2 * tiles, m), BF16),
            pltpu.VMEM((2 * nb, 128), F32),
            pltpu.VMEM((2 * mb, 128), F32),
            pltpu.VMEM((nb, 128), F32),
            pltpu.VMEM((mb, 128), F32),
            pltpu.VMEM((nb, 128), F32),
            pltpu.VMEM((mb, 128), F32),
            pltpu.VMEM((NX, 2 * nb, 128), BF16),
            pltpu.VMEM((NZ, 2 * nb, 128), BF16),
            pltpu.VMEM((NR, 2 * mb, 128), BF16),
            pltpu.VMEM((2, NX, nb, 128), BF16),
            pltpu.VMEM((2, NZ, nb, 128), BF16),
            pltpu.VMEM((2, NR, mb, 128), F32),
            dma((5,)),
            dma((NZ, NX)),
            dma((NZ, NX)),
            dma((NZ,)),
            dma((NZ,)),
            dma((3, NX)),
            dma((3, NX)),
            dma((3, NZ)),
            dma((3, NZ)),
            dma((3, NR)),
            dma((3, NR)),
        ],
        compiler_params=pltpu.CompilerParams(
            collective_id=0, has_side_effects=True, vmem_limit_bytes=50 * 1024 * 1024
        ),
    )(logged, targets, log_a.reshape(nb, 128), log_b.reshape(1, m), start_g.reshape(1, m))
    return f.reshape(n), g.reshape(m)


def solution(mesh):
    placed = (P(("rows", "cols"), None), P("cols", None), P("rows"), P("cols"), P("cols"))
    return jax.shard_map(
        local, mesh=mesh, in_specs=placed, out_specs=(P("rows"), P("cols")), check_vma=False
    )
```

```python
import functools

import jax
import jax.numpy as jnp
from jax import lax
from jax.experimental import pallas as pl
from jax.experimental.pallas import tpu as pltpu
from jax.sharding import PartitionSpec as P

NX, NZ, NR = 4, 8, 8
F32, BF16 = jnp.float32, jnp.bfloat16
BENT = (1, 7, 2, 6)
NT = (((1,), (1,)), ((), ()))
TI = 256
TJ = 256
WIDE = 512
MESH = pl.DeviceIdType.MESH


def dot(a, b, dims=(((1,), (0,)), ((), ()))):
    return lax.dot_general(a, b, dims, preferred_element_type=F32)


def flat(ref, rows, start=0):
    return jnp.concatenate([ref[start + k : start + k + 1, :] for k in range(rows)], axis=1)


def put(ref, value, start=0):
    for k in range(value.shape[1] // 128):
        ref[start + k : start + k + 1, :] = value[:, k * 128 : (k + 1) * 128]


def pieces(value, count):
    out = []
    for k in range(count):
        part = value.astype(BF16).astype(F32)
        out.append(part)
        value = value - part
    return out


def stack_pieces(value, count, rows=16):
    n = value.shape[1]
    index = lax.broadcasted_iota(jnp.int32, (rows, n), 0)
    out = jnp.zeros((rows, n), F32)
    for k, part in enumerate(pieces(value, count)):
        out = jnp.where(index == k, jnp.broadcast_to(part, (rows, n)), out)
    return out.astype(BF16)


def selector(rows, count):
    return (lax.broadcasted_iota(jnp.int32, (rows, 128), 1) < count).astype(F32).astype(BF16)


def square_sums(block):
    wide = block.astype(F32)
    high, low = pieces(wide * wide, 2)
    ones = jnp.ones((8, block.shape[1]), BF16)
    total = dot(ones, high.astype(BF16), NT) + dot(ones, low.astype(BF16), NT)
    return total[0:1, :]


def columns_of(stacked, eye):
    return dot(eye, stacked, NT).astype(BF16)


def kernel(
    x_hbm, y_hbm, la_hbm, lb_hbm, g_hbm, f_out, g_out,
    y_ref, la_ref, lb_ref, g_ref,
    xv, ya, p, held, eye, sel, best_col, sum_col, w, alpha, rowpart, colpart, rowstat, colstat, xn, yn, v1, lse,
    xpair, zpair, rpair, xbuf, zbuf, rbuf, local_sem,
    gx_send, gx_recv, gz_send, gz_recv, x_send, x_recv, z_send, z_recv, r_send, r_recv,
):
    n, m = xv.shape[0], ya.shape[0]
    nb, mb = n // 128, m // 128
    tiles = n // TI
    row = lax.axis_index("rows")
    col = lax.axis_index("cols")
    px, pz = col // NZ, lax.rem(col, NZ)

    def at_x(k):
        return (row, lax.rem(px + k, NX) * NZ + pz)

    def at_z(k):
        return (row, px * NZ + lax.rem(pz + k, NZ))

    def at_r(k):
        return (lax.rem(row + k, NR), col)

    barrier = pltpu.get_barrier_semaphore()
    for at, count in ((at_x, NX), (at_z, NZ), (at_r, NR)):
        for k in range(1, count):
            pl.semaphore_signal(barrier, inc=1, device_id=at(k), device_id_type=MESH)

    own_rows = pl.ds(pl.multiple_of(col * 128, 128), 128)
    moves = (
        (x_hbm, xv.at[own_rows, pl.ds(0, 128)]), (y_hbm, y_ref), (la_hbm, la_ref), (lb_hbm, lb_ref), (g_hbm, g_ref),
    )
    fetch = [pltpu.make_async_copy(src, dst, local_sem.at[k]) for k, (src, dst) in enumerate(moves)]
    for one in fetch:
        one.start()
    index = lax.broadcasted_iota(jnp.int32, (TI, TI), 0) == lax.broadcasted_iota(jnp.int32, (TI, TI), 1)
    eye[...] = jnp.where(index, 1.0, 0.0).astype(BF16)
    sel[...] = selector(sel.shape[0], 3)
    ya[:, 128:256] = jnp.zeros((m, 128), BF16)
    xv[:, 128:256] = jnp.zeros((n, 128), BF16)
    for one in fetch:
        one.wait()

    for k in range(m // TI):
        cut = pl.ds(k * TI, TI)
        block = y_ref[cut, :]
        ya[cut, 0:128] = (block.astype(F32) * 4.0).astype(BF16)
        norm = square_sums(block)
        put(yn, norm, 2 * k)
        u = lb_ref[:, cut] + 2.0 * g_ref[:, cut] - 2.0 * norm
        ya[cut, 128:144] = columns_of(stack_pieces(u, 3), eye[...])

    pl.semaphore_wait(barrier, NX + NZ + NR - 3)

    def remote(src, dst, send, recv, device):
        return pltpu.make_async_remote_copy(
            src_ref=src, dst_ref=dst, send_sem=send, recv_sem=recv, device_id=device, device_id_type=MESH
        )

    def came_x(s):
        return lax.rem(px + NX - s, NX)

    def came_z(k):
        return lax.rem(pz + NZ - k, NZ)

    def shard_rows(cx, cz):
        return pl.ds(pl.multiple_of((cx * NZ + cz) * 128, 128), 128)

    def shard(cx, cz):
        return xv.at[shard_rows(cx, cz), pl.ds(0, 128)]

    def z_copy(k):
        own = shard(px, pz)
        return remote(own, own, gz_send.at[k], gz_recv.at[k], at_z(k))

    def x_copy(k, s):
        block = shard(px, came_z(k))
        return remote(block, block, gx_send.at[k, s], gx_recv.at[k, s], at_x(s))

    def turn(q):
        odd = lax.rem(q, 2)
        return odd * ((q + 1) // 2) + (1 - odd) * lax.rem(NZ - q // 2, NZ)

    for s in range(1, NX):
        x_copy(0, s).start()
    for q in range(1, NZ):
        z_copy((q + 1) // 2 if q % 2 else NZ - q // 2).start()
    def bent_copy(k):
        block = shard(came_x(2), pz)
        return remote(block, block, gx_send.at[k, 2], gx_recv.at[k, 2], at_z(k))

    def forward(q):
        k = turn(q)
        z_copy(k).wait_recv()
        x_copy(k, 1).start()
        x_copy(k, 3).start()

        @pl.when(q > len(BENT))
        def opposite():
            x_copy(k, 2).start()

    def pass_1(q, carry):
        @pl.when(q < NZ - 2)
        def ahead():
            forward(q + 2)

        k = turn(q)
        for s in range(1, NX):
            remote(shard(came_x(s), came_z(k)), shard(came_x(s), came_z(k)), gx_send.at[k, s], gx_recv.at[k, s],
                   at_x(s)).wait_recv()

        @pl.when(q == 0)
        def bent():
            for distance in BENT:
                bent_copy(distance).start()

        points = jnp.concatenate([xv[shard_rows(came_x(s), came_z(k)), 0:128] for s in range(NX)], axis=0)
        points = jnp.concatenate([points, sel[0 : NX * 128, :]], axis=1)
        top = total = None
        for j in range(m // TJ):
            s = dot(ya[j * TJ : (j + 1) * TJ, :], points, NT).reshape(TJ // 8, 8, NX * 128)
            here = jnp.max(s, axis=0)
            if j == 0:
                top = here
                total = jnp.sum(jnp.exp(s - top[None]), axis=0)
            else:
                upper = jnp.maximum(top, here)
                total = total * jnp.exp(top - upper) + jnp.sum(jnp.exp(s - upper[None]), axis=0)
                top = upper
        best = jnp.max(top, axis=0, keepdims=True)
        whole = jnp.sum(total * jnp.exp(top - best), axis=0, keepdims=True)
        for start, value in ((0, best), (nb, whole)):
            for s in range(NX):
                rowstat[pl.ds(start + came_x(s) * NZ + came_z(k), 1), :] = value[:, s * 128 : (s + 1) * 128]
        return carry

    forward(1)
    lax.fori_loop(0, NZ, pass_1, 0)

    def spread(buf, send, recv, at, me, count):
        for k in range(1, count):
            remote(buf.at[me], buf.at[me], send.at[k], recv.at[k], at(k)).start()

    def collect(buf, send, recv, at, me, count):
        for k in range(1, count):
            remote(buf.at[me], buf.at[me], send.at[k], recv.at[k], at(k)).wait()

    def on_x(buf, slot):
        return (buf, x_send.at[slot], x_recv.at[slot], at_x, px, NX)

    def on_z(buf, slot):
        return (buf, z_send.at[slot], z_recv.at[slot], at_z, pz, NZ)

    def on_r(buf, slot):
        return (buf, r_send.at[slot], r_recv.at[slot], at_r, row, NR)

    def join(buf, count, size):
        tops = [buf[k, 0:size, :].astype(F32) for k in range(count)]
        sums = [buf[k, size : 2 * size, :].astype(F32) for k in range(count)]
        top = functools.reduce(jnp.maximum, tops)
        total = functools.reduce(lambda a, b: a + b, [s * jnp.exp(t - top) for t, s in zip(tops, sums)])
        return top, total

    def add(buf, count, size):
        return functools.reduce(lambda a, b: a + b, [buf[k, 0:size, :].astype(F32) for k in range(count)])

    def pack(ref, top, total):
        size = top.shape[0]
        near = top.astype(BF16)
        ref[0:size, :] = near
        ref[size : 2 * size, :] = (total * jnp.exp(top - near.astype(F32))).astype(BF16)

    def row_norms():
        def one(k, carry):
            norm = square_sums(xv[pl.ds(pl.multiple_of(k * TI, TI), TI), 0:128])
            xn[pl.ds(2 * k, 1), :] = norm[:, 0:128]
            xn[pl.ds(2 * k + 1, 1), :] = norm[:, 128:256]
            return carry

        lax.fori_loop(0, tiles, one, 0)

    pack(xpair.at[px], rowstat[0:nb, :], rowstat[nb : 2 * nb, :])
    spread(*on_x(xpair, 0))
    row_norms()
    collect(*on_x(xpair, 0))
    pack(zpair.at[pz], *join(xpair, NX, nb))
    spread(*on_z(zpair, 0))
    collect(*on_z(zpair, 0))
    top, total = join(zpair, NZ, nb)
    v1[...] = la_ref[...] - (top + jnp.log(total))
    alpha[...] = stack_pieces(flat(v1, nb), 3)

    def place(k, carry):
        cut = pl.ds(pl.multiple_of(k * TI, TI), TI)
        xv[cut, 128:144] = columns_of(alpha[:, cut], eye[...])
        return carry

    lax.fori_loop(0, tiles, place, 0)

    halves = range(2)
    nh, mh = n // 2, m // 2

    def block(q, carry):
        lanes = pl.ds(pl.multiple_of(q * WIDE, WIDE), WIDE)
        weights = jnp.concatenate([ya[lanes, 0:128], sel[...]], axis=1)
        top = None
        for t in range(tiles):
            s = dot(xv[t * TI : (t + 1) * TI, :], weights, NT)
            held[t * TI : (t + 1) * TI, :] = s
            here = jnp.max(s.reshape(TI // 8, 8, WIDE), axis=0)
            top = here if top is None else jnp.maximum(top, here)
        top = jnp.max(top, axis=0, keepdims=True)
        total = jnp.zeros((8, WIDE), F32)
        for t in range(tiles):
            e = jnp.exp(held[t * TI : (t + 1) * TI, :].reshape(TI // 8, 8, WIDE) - top[None])
            total = total + jnp.sum(e, axis=0)
            p[t * TI : (t + 1) * TI, lanes] = e.reshape(TI, WIDE).astype(BF16)
        best_col[:, lanes] = top
        sum_col[:, lanes] = jnp.sum(total, axis=0, keepdims=True)
        return carry

    for c in halves:
        lax.fori_loop(c * (mh // WIDE), (c + 1) * (mh // WIDE), block, 0)
        put(rpair.at[c, row], best_col[:, c * mh : (c + 1) * mh])
        put(rpair.at[c, row], sum_col[:, c * mh : (c + 1) * mh], mb // 2)
        spread(*on_r(rpair.at[c], c))

    def col_half(c):
        return slice(c * mh, (c + 1) * mh), slice(c * (mb // 2), (c + 1) * (mb // 2))

    def row_half(h):
        return slice(h * nh, (h + 1) * nh), slice(h * (nb // 2), (h + 1) * (nb // 2))

    def scale_of(step, c):
        lanes, rows = col_half(c)
        if step == 1:
            collect(*on_r(rpair.at[c], c))
            top, total = join(rpair.at[c], NR, mb // 2)
            lse[rows, :] = top + jnp.log(total)
            w[:, lanes] = jnp.exp(best_col[:, lanes] - flat(lse, mb // 2, c * (mb // 2)))
            return jnp.exp(lb_ref[:, lanes]) * w[:, lanes]
        collect(*on_r(rbuf.at[0, c], 2 + c))
        colstat[rows, :] = add(rbuf.at[0, c], NR, mb // 2)
        return jnp.exp(lb_ref[:, lanes]) * w[:, lanes] / flat(colstat, mb // 2, c * (mb // 2))

    for step in (1, 2):
        for c in halves:
            lanes = col_half(c)[0]
            beta = stack_pieces(scale_of(step, c), 2)
            if c == 0:
                rowpart[...] = dot(beta, p[:, lanes], NT)[0:8, :]
            else:
                for h in halves:
                    cut, rows = row_half(h)
                    out = rowpart[:, cut] + dot(beta, p[cut, lanes], NT)[0:8, :]
                    put(rowstat, jnp.sum(out, axis=0, keepdims=True), h * (nb // 2))
                    xbuf[step - 1, h, px] = rowstat[rows, :].astype(BF16)
                    spread(*on_x(xbuf.at[step - 1, h], 2 * step + h))
        for h in halves:
            collect(*on_x(xbuf.at[step - 1, h], 2 * step + h))
            zbuf[step - 1, h, pz] = add(xbuf.at[step - 1, h], NX, nb // 2).astype(BF16)
            spread(*on_z(zbuf.at[step - 1, h], 2 * step + h))
        for h in halves:
            cut, rows = row_half(h)
            collect(*on_z(zbuf.at[step - 1, h], 2 * step + h))
            rowsum = add(zbuf.at[step - 1, h], NZ, nb // 2)
            rowstat[rows, :] = jnp.exp(la_ref[rows, :]) / rowsum
            if step == 2:
                f_out[rows, :] = xn[rows, :] + 0.5 * (v1[rows, :] - jnp.log(rowsum))
            share = stack_pieces(flat(rowstat, nb // 2, h * (nb // 2)), 2)
            if h == 0:
                colpart[...] = dot(share, p[cut, :])[0:8, :]
            else:
                for c in halves:
                    lanes = col_half(c)[0]
                    out = colpart[:, lanes] + dot(share, p[cut, lanes])[0:8, :]
                    put(rbuf.at[step - 1, c, row], jnp.sum(out, axis=0, keepdims=True) * w[:, lanes])
                    spread(*on_r(rbuf.at[step - 1, c], 2 * step + c))
    for c in halves:
        rows = col_half(c)[1]
        collect(*on_r(rbuf.at[1, c], 4 + c))
        g_out[rows, :] = yn[rows, :] - 0.5 * (lse[rows, :] + jnp.log(add(rbuf.at[1, c], NR, mb // 2)))

    for k in range(NZ):
        if k:
            z_copy(k).wait_send()
        for s in range(1, NX):
            (bent_copy(k) if s == 2 and k in BENT else x_copy(k, s)).wait_send()


def local(logged, targets, log_a, log_b, start_g):
    n, m = log_a.shape[0], log_b.shape[0]
    nb, mb = n // 128, m // 128
    tiles = n // TI
    dma = pltpu.SemaphoreType.DMA
    vmem = pl.BlockSpec(memory_space=pltpu.VMEM)
    anywhere = pl.BlockSpec(memory_space=pltpu.HBM)
    f, g = pl.pallas_call(
        kernel,
        out_shape=(jax.ShapeDtypeStruct((nb, 128), F32), jax.ShapeDtypeStruct((mb, 128), F32)),
        in_specs=[anywhere] * 5,
        out_specs=(vmem, vmem),
        scratch_shapes=[
            pltpu.VMEM((m, 128), BF16),
            pltpu.VMEM((nb, 128), F32),
            pltpu.VMEM((1, m), F32),
            pltpu.VMEM((1, m), F32),
            pltpu.VMEM((n, 256), BF16),
            pltpu.VMEM((m, 256), BF16),
            pltpu.VMEM((n, m), BF16),
            pltpu.VMEM((n, WIDE), F32),
            pltpu.VMEM((TI, TI), BF16),
            pltpu.VMEM((WIDE, 128), BF16),
            pltpu.VMEM((1, m), F32),
            pltpu.VMEM((1, m), F32),
            pltpu.VMEM((1, m), F32),
            pltpu.VMEM((16, n), BF16),
            pltpu.VMEM((8, n), F32),
            pltpu.VMEM((8, m), F32),
            pltpu.VMEM((2 * nb, 128), F32),
            pltpu.VMEM((mb, 128), F32),
            pltpu.VMEM((nb, 128), F32),
            pltpu.VMEM((mb, 128), F32),
            pltpu.VMEM((nb, 128), F32),
            pltpu.VMEM((mb, 128), F32),
            pltpu.VMEM((NX, 2 * nb, 128), BF16),
            pltpu.VMEM((NZ, 2 * nb, 128), BF16),
            pltpu.VMEM((2, NR, mb, 128), F32),
            pltpu.VMEM((2, 2, NX, nb // 2, 128), BF16),
            pltpu.VMEM((2, 2, NZ, nb // 2, 128), BF16),
            pltpu.VMEM((2, 2, NR, mb // 2, 128), F32),
            dma((5,)),
            dma((NZ, NX)),
            dma((NZ, NX)),
            dma((NZ,)),
            dma((NZ,)),
            dma((6, NX)),
            dma((6, NX)),
            dma((6, NZ)),
            dma((6, NZ)),
            dma((6, NR)),
            dma((6, NR)),
        ],
        compiler_params=pltpu.CompilerParams(
            collective_id=0, has_side_effects=True, vmem_limit_bytes=64 * 1024 * 1024
        ),
    )(logged, targets, log_a.reshape(nb, 128), log_b.reshape(1, m), start_g.reshape(1, m))
    return f.reshape(n), g.reshape(m)


def solution(mesh):
    placed = (P(("rows", "cols"), None), P("cols", None), P("rows"), P("cols"), P("cols"))
    return jax.shard_map(
        local, mesh=mesh, in_specs=placed, out_specs=(P("rows"), P("cols")), check_vma=False
    )
```

```python
import functools

import jax
import jax.numpy as jnp
from jax import lax
from jax.experimental import pallas as pl
from jax.experimental.pallas import tpu as pltpu
from jax.sharding import PartitionSpec as P

NX, NZ, NR = 4, 8, 8
F32, BF16 = jnp.float32, jnp.bfloat16
BENT = (1, 7, 2, 6)
NT = (((1,), (1,)), ((), ()))
TI = 256
TJ = 256
WIDE = 512
QUARTERS = 4
MESH = pl.DeviceIdType.MESH


def dot(a, b, dims=(((1,), (0,)), ((), ()))):
    return lax.dot_general(a, b, dims, preferred_element_type=F32)


def flat(ref, rows, start=0):
    return jnp.concatenate([ref[start + k : start + k + 1, :] for k in range(rows)], axis=1)


def put(ref, value, start=0):
    for k in range(value.shape[1] // 128):
        ref[start + k : start + k + 1, :] = value[:, k * 128 : (k + 1) * 128]


def pieces(value, count):
    out = []
    for k in range(count):
        part = value.astype(BF16).astype(F32)
        out.append(part)
        value = value - part
    return out


def stack_pieces(value, count, rows=16):
    n = value.shape[1]
    index = lax.broadcasted_iota(jnp.int32, (rows, n), 0)
    out = jnp.zeros((rows, n), F32)
    for k, part in enumerate(pieces(value, count)):
        out = jnp.where(index == k, jnp.broadcast_to(part, (rows, n)), out)
    return out.astype(BF16)


def selector(rows, count):
    return (lax.broadcasted_iota(jnp.int32, (rows, 128), 1) < count).astype(F32).astype(BF16)


def square_sums(block):
    wide = block.astype(F32)
    high, low = pieces(wide * wide, 2)
    ones = jnp.ones((8, block.shape[1]), BF16)
    total = dot(ones, high.astype(BF16), NT) + dot(ones, low.astype(BF16), NT)
    return total[0:1, :]


def columns_of(stacked, eye):
    return dot(eye, stacked, NT).astype(BF16)


def kernel(
    x_hbm, y_hbm, la_hbm, lb_hbm, g_hbm, out,
    y_ref, la_ref, lb_ref, g_ref,
    xv, ya, p, held, eye, sel, best_col, sum_col, w, alpha, rowpart, colpart, rowstat, colstat, xn, yn, v1, lse,
    xpair, zpair, rpair, xbuf, zbuf, rbuf, local_sem,
    gx_send, gx_recv, gz_send, gz_recv, x_send, x_recv, z_send, z_recv, r_send, r_recv,
):
    n, m = xv.shape[0], ya.shape[0]
    nb, mb = n // 128, m // 128
    tiles = n // TI
    row = lax.axis_index("rows")
    col = lax.axis_index("cols")
    px, pz = col // NZ, lax.rem(col, NZ)

    def at_x(k):
        return (row, lax.rem(px + k, NX) * NZ + pz)

    def at_z(k):
        return (row, px * NZ + lax.rem(pz + k, NZ))

    def at_r(k):
        return (lax.rem(row + k, NR), col)

    barrier = pltpu.get_barrier_semaphore()
    for at, count in ((at_x, NX), (at_z, NZ), (at_r, NR)):
        for k in range(1, count):
            pl.semaphore_signal(barrier, inc=1, device_id=at(k), device_id_type=MESH)

    own_rows = pl.ds(pl.multiple_of(col * 128, 128), 128)
    moves = (
        (x_hbm, xv.at[own_rows, pl.ds(0, 128)]), (y_hbm, y_ref), (la_hbm, la_ref), (lb_hbm, lb_ref), (g_hbm, g_ref),
    )
    fetch = [pltpu.make_async_copy(src, dst, local_sem.at[k]) for k, (src, dst) in enumerate(moves)]
    for one in fetch:
        one.start()
    index = lax.broadcasted_iota(jnp.int32, (TI, TI), 0) == lax.broadcasted_iota(jnp.int32, (TI, TI), 1)
    eye[...] = jnp.where(index, 1.0, 0.0).astype(BF16)
    sel[...] = selector(sel.shape[0], 3)
    ya[:, 128:256] = jnp.zeros((m, 128), BF16)
    xv[:, 128:256] = jnp.zeros((n, 128), BF16)
    fetch[0].wait()
    pl.semaphore_wait(barrier, NX + NZ + NR - 3)

    def remote(src, dst, send, recv, device):
        return pltpu.make_async_remote_copy(
            src_ref=src, dst_ref=dst, send_sem=send, recv_sem=recv, device_id=device, device_id_type=MESH
        )

    def came_x(s):
        return lax.rem(px + NX - s, NX)

    def came_z(k):
        return lax.rem(pz + NZ - k, NZ)

    def shard_rows(cx, cz):
        return pl.ds(pl.multiple_of((cx * NZ + cz) * 128, 128), 128)

    def shard(cx, cz):
        return xv.at[shard_rows(cx, cz), pl.ds(0, 128)]

    def z_copy(k):
        own = shard(px, pz)
        return remote(own, own, gz_send.at[k], gz_recv.at[k], at_z(k))

    def x_copy(k, s):
        block = shard(px, came_z(k))
        return remote(block, block, gx_send.at[k, s], gx_recv.at[k, s], at_x(s))

    def turn(q):
        odd = lax.rem(q, 2)
        return odd * ((q + 1) // 2) + (1 - odd) * lax.rem(NZ - q // 2, NZ)

    for s in range(1, NX):
        x_copy(0, s).start()
    for q in range(1, NZ):
        z_copy((q + 1) // 2 if q % 2 else NZ - q // 2).start()
    for one in fetch[1:]:
        one.wait()

    for k in range(m // TI):
        cut = pl.ds(k * TI, TI)
        block = y_ref[cut, :]
        ya[cut, 0:128] = (block.astype(F32) * 4.0).astype(BF16)
        norm = square_sums(block)
        put(yn, norm, 2 * k)
        u = lb_ref[:, cut] + 2.0 * g_ref[:, cut] - 2.0 * norm
        ya[cut, 128:144] = columns_of(stack_pieces(u, 3), eye[...])

    def bent_copy(k):
        block = shard(came_x(2), pz)
        return remote(block, block, gx_send.at[k, 2], gx_recv.at[k, 2], at_z(k))

    def forward(q):
        k = turn(q)
        z_copy(k).wait_recv()
        x_copy(k, 1).start()
        x_copy(k, 3).start()

        @pl.when(q > len(BENT))
        def opposite():
            x_copy(k, 2).start()

    def pass_1(q, carry):
        @pl.when(q < NZ - 2)
        def ahead():
            forward(q + 2)

        k = turn(q)
        for s in range(1, NX):
            remote(shard(came_x(s), came_z(k)), shard(came_x(s), came_z(k)), gx_send.at[k, s], gx_recv.at[k, s],
                   at_x(s)).wait_recv()

        @pl.when(q == 0)
        def bent():
            for distance in BENT:
                bent_copy(distance).start()

        points = jnp.concatenate([xv[shard_rows(came_x(s), came_z(k)), 0:128] for s in range(NX)], axis=0)
        points = jnp.concatenate([points, sel[0 : NX * 128, :]], axis=1)
        top = total = None
        for j in range(m // TJ):
            s = dot(ya[j * TJ : (j + 1) * TJ, :], points, NT).reshape(TJ // 8, 8, NX * 128)
            here = jnp.max(s, axis=0)
            if j == 0:
                top = here
                total = jnp.sum(jnp.exp(s - top[None]), axis=0)
            else:
                upper = jnp.maximum(top, here)
                total = total * jnp.exp(top - upper) + jnp.sum(jnp.exp(s - upper[None]), axis=0)
                top = upper
        best = jnp.max(top, axis=0, keepdims=True)
        whole = jnp.sum(total * jnp.exp(top - best), axis=0, keepdims=True)
        for start, value in ((0, best), (nb, whole)):
            for s in range(NX):
                rowstat[pl.ds(start + came_x(s) * NZ + came_z(k), 1), :] = value[:, s * 128 : (s + 1) * 128]
        return carry

    forward(1)
    lax.fori_loop(0, NZ, pass_1, 0)

    def spread(buf, send, recv, at, me, count):
        for k in range(1, count):
            remote(buf.at[me], buf.at[me], send.at[k], recv.at[k], at(k)).start()

    def collect(buf, send, recv, at, me, count):
        for k in range(1, count):
            remote(buf.at[me], buf.at[me], send.at[k], recv.at[k], at(k)).wait()

    def on_x(buf, slot):
        return (buf, x_send.at[slot], x_recv.at[slot], at_x, px, NX)

    def on_z(buf, slot):
        return (buf, z_send.at[slot], z_recv.at[slot], at_z, pz, NZ)

    def on_r(buf, slot):
        return (buf, r_send.at[slot], r_recv.at[slot], at_r, row, NR)

    def join(buf, count, size):
        tops = [buf[k, 0:size, :].astype(F32) for k in range(count)]
        sums = [buf[k, size : 2 * size, :].astype(F32) for k in range(count)]
        top = functools.reduce(jnp.maximum, tops)
        total = functools.reduce(lambda a, b: a + b, [s * jnp.exp(t - top) for t, s in zip(tops, sums)])
        return top, total

    def add(buf, count, size):
        return functools.reduce(lambda a, b: a + b, [buf[k, 0:size, :].astype(F32) for k in range(count)])

    def pack(ref, top, total):
        size = top.shape[0]
        near = top.astype(BF16)
        ref[0:size, :] = near
        ref[size : 2 * size, :] = (total * jnp.exp(top - near.astype(F32))).astype(BF16)

    def row_norms():
        def one(k, carry):
            norm = square_sums(xv[pl.ds(pl.multiple_of(k * TI, TI), TI), 0:128])
            xn[pl.ds(2 * k, 1), :] = norm[:, 0:128]
            xn[pl.ds(2 * k + 1, 1), :] = norm[:, 128:256]
            return carry

        lax.fori_loop(0, tiles, one, 0)

    pack(xpair.at[px], rowstat[0:nb, :], rowstat[nb : 2 * nb, :])
    spread(*on_x(xpair, 0))
    row_norms()
    collect(*on_x(xpair, 0))
    pack(zpair.at[pz], *join(xpair, NX, nb))
    spread(*on_z(zpair, 0))
    collect(*on_z(zpair, 0))
    top, total = join(zpair, NZ, nb)
    v1[...] = la_ref[...] - (top + jnp.log(total))
    alpha[...] = stack_pieces(flat(v1, nb), 3)

    def place(k, carry):
        cut = pl.ds(pl.multiple_of(k * TI, TI), TI)
        xv[cut, 128:144] = columns_of(alpha[:, cut], eye[...])
        return carry

    lax.fori_loop(0, tiles, place, 0, unroll=8)

    halves = range(2)
    nh, mh = n // 2, m // 2

    def block(q, carry):
        lanes = pl.ds(pl.multiple_of(q * WIDE, WIDE), WIDE)
        weights = jnp.concatenate([ya[lanes, 0:128], sel[...]], axis=1)
        top = None
        for t in range(tiles):
            s = dot(xv[t * TI : (t + 1) * TI, :], weights, NT)
            held[t * TI : (t + 1) * TI, :] = s
            here = jnp.max(s.reshape(TI // 8, 8, WIDE), axis=0)
            top = here if top is None else jnp.maximum(top, here)
        top = jnp.max(top, axis=0, keepdims=True)
        total = jnp.zeros((8, WIDE), F32)
        for t in range(tiles):
            e = jnp.exp(held[t * TI : (t + 1) * TI, :].reshape(TI // 8, 8, WIDE) - top[None])
            total = total + jnp.sum(e, axis=0)
            p[t * TI : (t + 1) * TI, lanes] = e.reshape(TI, WIDE).astype(BF16)
        best_col[:, lanes] = top
        sum_col[:, lanes] = jnp.sum(total, axis=0, keepdims=True)
        return carry

    def columns(c, count):
        lanes, rows = m // count, mb // count
        return slice(c * lanes, (c + 1) * lanes), slice(c * rows, (c + 1) * rows), rows

    for c in range(QUARTERS):
        lanes, _, size = columns(c, QUARTERS)
        lax.fori_loop(c * (m // QUARTERS // WIDE), (c + 1) * (m // QUARTERS // WIDE), block, 0)
        put(rpair.at[c, row], best_col[:, lanes])
        put(rpair.at[c, row], sum_col[:, lanes], size)
        spread(*on_r(rpair.at[c], c))

    def row_half(h):
        return slice(h * nh, (h + 1) * nh), slice(h * (nb // 2), (h + 1) * (nb // 2))

    def scale_of(step, c):
        count = QUARTERS if step == 1 else 2
        lanes, rows, size = columns(c, count)
        if step == 1:
            collect(*on_r(rpair.at[c], c))
            top, total = join(rpair.at[c], NR, size)
            lse[rows, :] = top + jnp.log(total)
            w[:, lanes] = jnp.exp(best_col[:, lanes] - flat(lse, size, c * size))
            return jnp.exp(lb_ref[:, lanes]) * w[:, lanes]
        collect(*on_r(rbuf.at[0, c], QUARTERS + c))
        colstat[rows, :] = add(rbuf.at[0, c], NR, size)
        return jnp.exp(lb_ref[:, lanes]) * w[:, lanes] / flat(colstat, size, c * size)

    for step in (1, 2):
        count = QUARTERS if step == 1 else 2
        for c in range(count):
            lanes = columns(c, count)[0]
            beta = stack_pieces(scale_of(step, c), 2)
            if c == 0:
                rowpart[...] = dot(beta, p[:, lanes], NT)[0:8, :]
            elif c < count - 1:
                rowpart[...] = rowpart[...] + dot(beta, p[:, lanes], NT)[0:8, :]
            else:
                for h in halves:
                    cut, rows = row_half(h)
                    both = rowpart[:, cut] + dot(beta, p[cut, lanes], NT)[0:8, :]
                    put(rowstat, jnp.sum(both, axis=0, keepdims=True), h * (nb // 2))
                    xbuf[step - 1, h, px] = rowstat[rows, :].astype(BF16)
                    spread(*on_x(xbuf.at[step - 1, h], 2 * step + h))
        for h in halves:
            collect(*on_x(xbuf.at[step - 1, h], 2 * step + h))
            zbuf[step - 1, h, pz] = add(xbuf.at[step - 1, h], NX, nb // 2).astype(BF16)
            spread(*on_z(zbuf.at[step - 1, h], 2 * step + h))
        for h in halves:
            cut, rows = row_half(h)
            collect(*on_z(zbuf.at[step - 1, h], 2 * step + h))
            rowsum = add(zbuf.at[step - 1, h], NZ, nb // 2)
            rowstat[rows, :] = jnp.exp(la_ref[rows, :]) / rowsum
            if step == 2:
                out[rows, :] = xn[rows, :] + 0.5 * (v1[rows, :] - jnp.log(rowsum))
            share = stack_pieces(flat(rowstat, nb // 2, h * (nb // 2)), 2)
            if h == 0:
                colpart[...] = dot(share, p[cut, :])[0:8, :]
            else:
                for c in halves:
                    lanes = columns(c, 2)[0]
                    both = colpart[:, lanes] + dot(share, p[cut, lanes])[0:8, :]
                    put(rbuf.at[step - 1, c, row], jnp.sum(both, axis=0, keepdims=True) * w[:, lanes])
                    spread(*on_r(rbuf.at[step - 1, c], QUARTERS + 2 * (step - 1) + c))
    for c in halves:
        rows = columns(c, 2)[1]
        collect(*on_r(rbuf.at[1, c], QUARTERS + 2 + c))
        out[nb + c * (mb // 2) : nb + (c + 1) * (mb // 2), :] = yn[rows, :] - 0.5 * (lse[rows, :] + jnp.log(add(rbuf.at[1, c], NR, mb // 2)))

    for k in range(NZ):
        if k:
            z_copy(k).wait_send()
        for s in range(1, NX):
            (bent_copy(k) if s == 2 and k in BENT else x_copy(k, s)).wait_send()


def local(logged, targets, log_a, log_b, start_g):
    n, m = log_a.shape[0], log_b.shape[0]
    nb, mb = n // 128, m // 128
    tiles = n // TI
    dma = pltpu.SemaphoreType.DMA
    vmem = pl.BlockSpec(memory_space=pltpu.VMEM)
    anywhere = pl.BlockSpec(memory_space=pltpu.HBM)
    out = pl.pallas_call(
        kernel,
        out_shape=jax.ShapeDtypeStruct((nb + mb, 128), F32),
        in_specs=[anywhere] * 5,
        out_specs=vmem,
        scratch_shapes=[
            pltpu.VMEM((m, 128), BF16),
            pltpu.VMEM((nb, 128), F32),
            pltpu.VMEM((1, m), F32),
            pltpu.VMEM((1, m), F32),
            pltpu.VMEM((n, 256), BF16),
            pltpu.VMEM((m, 256), BF16),
            pltpu.VMEM((n, m), BF16),
            pltpu.VMEM((n, WIDE), F32),
            pltpu.VMEM((TI, TI), BF16),
            pltpu.VMEM((WIDE, 128), BF16),
            pltpu.VMEM((1, m), F32),
            pltpu.VMEM((1, m), F32),
            pltpu.VMEM((1, m), F32),
            pltpu.VMEM((16, n), BF16),
            pltpu.VMEM((8, n), F32),
            pltpu.VMEM((8, m), F32),
            pltpu.VMEM((2 * nb, 128), F32),
            pltpu.VMEM((mb, 128), F32),
            pltpu.VMEM((nb, 128), F32),
            pltpu.VMEM((mb, 128), F32),
            pltpu.VMEM((nb, 128), F32),
            pltpu.VMEM((mb, 128), F32),
            pltpu.VMEM((NX, 2 * nb, 128), BF16),
            pltpu.VMEM((NZ, 2 * nb, 128), BF16),
            pltpu.VMEM((QUARTERS, NR, 2 * mb // QUARTERS, 128), F32),
            pltpu.VMEM((2, 2, NX, nb // 2, 128), BF16),
            pltpu.VMEM((2, 2, NZ, nb // 2, 128), BF16),
            pltpu.VMEM((2, 2, NR, mb // 2, 128), F32),
            dma((5,)),
            dma((NZ, NX)),
            dma((NZ, NX)),
            dma((NZ,)),
            dma((NZ,)),
            dma((6, NX)),
            dma((6, NX)),
            dma((6, NZ)),
            dma((6, NZ)),
            dma((QUARTERS + 4, NR)),
            dma((QUARTERS + 4, NR)),
        ],
        compiler_params=pltpu.CompilerParams(
            collective_id=0, has_side_effects=True, vmem_limit_bytes=64 * 1024 * 1024
        ),
    )(logged, targets, log_a.reshape(nb, 128), log_b.reshape(1, m), start_g.reshape(1, m))
    return out[:nb].reshape(n), out[nb:].reshape(m)


def solution(mesh):
    placed = (P(("rows", "cols"), None), P("cols", None), P("rows"), P("cols"), P("cols"))
    return jax.shard_map(
        local, mesh=mesh, in_specs=placed, out_specs=(P("rows"), P("cols")), check_vma=False
    )
```

```python
import functools

import jax
import jax.numpy as jnp
from jax import lax
from jax.experimental import pallas as pl
from jax.experimental.pallas import tpu as pltpu
from jax.sharding import PartitionSpec as P

NX, NZ, NR = 4, 8, 8
F32, BF16 = jnp.float32, jnp.bfloat16
AHEAD = 4
NT = (((1,), (1,)), ((), ()))
TI = 256
TJ = 256
WIDE = 512
QUARTERS = 4
MESH = pl.DeviceIdType.MESH


def dot(a, b, dims=(((1,), (0,)), ((), ()))):
    return lax.dot_general(a, b, dims, preferred_element_type=F32)


def flat(ref, rows, start=0):
    return jnp.concatenate([ref[start + k : start + k + 1, :] for k in range(rows)], axis=1)


def put(ref, value, start=0):
    for k in range(value.shape[1] // 128):
        ref[start + k : start + k + 1, :] = value[:, k * 128 : (k + 1) * 128]


def pieces(value, count):
    out = []
    for k in range(count):
        part = value.astype(BF16).astype(F32)
        out.append(part)
        value = value - part
    return out


def stack_pieces(value, count, rows=16):
    n = value.shape[1]
    index = lax.broadcasted_iota(jnp.int32, (rows, n), 0)
    out = jnp.zeros((rows, n), F32)
    for k, part in enumerate(pieces(value, count)):
        out = jnp.where(index == k, jnp.broadcast_to(part, (rows, n)), out)
    return out.astype(BF16)


def selector(rows, count):
    return (lax.broadcasted_iota(jnp.int32, (rows, 128), 1) < count).astype(F32).astype(BF16)


def square_sums(block):
    wide = block.astype(F32)
    high, low = pieces(wide * wide, 2)
    ones = jnp.ones((8, block.shape[1]), BF16)
    total = dot(ones, high.astype(BF16), NT) + dot(ones, low.astype(BF16), NT)
    return total[0:1, :]


def columns_of(stacked, eye):
    return dot(eye, stacked, NT).astype(BF16)


def kernel(
    x_hbm, y_hbm, la_hbm, lb_hbm, g_hbm, f_out, g_out,
    y_ref, la_ref, lb_ref, g_ref,
    xv, ya, p, held, eye, sel, best_col, sum_col, w, alpha, rowpart, colpart, rowstat, colstat, xn, yn, v1, lse,
    xpair, zpair, rpair, xbuf, zbuf, rbuf, local_sem,
    gx_send, gx_recv, gz_send, gz_recv, x_send, x_recv, z_send, z_recv, r_send, r_recv,
):
    n, m = xv.shape[0], ya.shape[0]
    nb, mb = n // 128, m // 128
    tiles = n // TI
    row = lax.axis_index("rows")
    col = lax.axis_index("cols")
    px, pz = col // NZ, lax.rem(col, NZ)

    def at_x(k):
        return (row, lax.rem(px + k, NX) * NZ + pz)

    def at_z(k):
        return (row, px * NZ + lax.rem(pz + k, NZ))

    def at_r(k):
        return (lax.rem(row + k, NR), col)

    barrier = pltpu.get_barrier_semaphore()
    for at, count in ((at_x, NX), (at_z, NZ), (at_r, NR)):
        for k in range(1, count):
            pl.semaphore_signal(barrier, inc=1, device_id=at(k), device_id_type=MESH)

    own_rows = pl.ds(pl.multiple_of(col * 128, 128), 128)
    moves = (
        (x_hbm, xv.at[own_rows, pl.ds(0, 128)]), (y_hbm, y_ref), (la_hbm, la_ref), (lb_hbm, lb_ref), (g_hbm, g_ref),
    )
    fetch = [pltpu.make_async_copy(src, dst, local_sem.at[k]) for k, (src, dst) in enumerate(moves)]
    for one in fetch:
        one.start()
    index = lax.broadcasted_iota(jnp.int32, (TI, TI), 0) == lax.broadcasted_iota(jnp.int32, (TI, TI), 1)
    eye[...] = jnp.where(index, 1.0, 0.0).astype(BF16)
    sel[...] = selector(sel.shape[0], 3)
    ya[:, 128:256] = jnp.zeros((m, 128), BF16)
    xv[:, 128:256] = jnp.zeros((n, 128), BF16)
    fetch[0].wait()
    pl.semaphore_wait(barrier, NX + NZ + NR - 3)

    def remote(src, dst, send, recv, device):
        return pltpu.make_async_remote_copy(
            src_ref=src, dst_ref=dst, send_sem=send, recv_sem=recv, device_id=device, device_id_type=MESH
        )

    def came_x(s):
        return lax.rem(px + NX - s, NX)

    def came_z(k):
        return lax.rem(pz + NZ - k, NZ)

    def shard_rows(cx, cz):
        return pl.ds(pl.multiple_of((cx * NZ + cz) * 128, 128), 128)

    def shard(cx, cz):
        return xv.at[shard_rows(cx, cz), pl.ds(0, 128)]

    def z_copy(k):
        own = shard(px, pz)
        return remote(own, own, gz_send.at[k], gz_recv.at[k], at_z(k))

    def x_copy(k, s):
        block = shard(px, came_z(k))
        return remote(block, block, gx_send.at[k, s], gx_recv.at[k, s], at_x(s))

    def turn(q):
        odd = lax.rem(q, 2)
        return odd * ((q + 1) // 2) + (1 - odd) * lax.rem(NZ - q // 2, NZ)

    for s in (1, 3, 2):
        x_copy(0, s).start()
    for q in range(1, NZ):
        z_copy((q + 1) // 2 if q % 2 else NZ - q // 2).start()
    for one in fetch[1:]:
        one.wait()

    for k in range(m // TI):
        cut = pl.ds(k * TI, TI)
        block = y_ref[cut, :]
        ya[cut, 0:128] = (block.astype(F32) * 4.0).astype(BF16)
        norm = square_sums(block)
        put(yn, norm, 2 * k)
        u = lb_ref[:, cut] + 2.0 * g_ref[:, cut] - 2.0 * norm
        ya[cut, 128:144] = columns_of(stack_pieces(u, 3), eye[...])

    def forward(q):
        k = turn(q)
        z_copy(k).wait_recv()
        for s in (1, 3, 2):
            x_copy(k, s).start()

    def pass_1(q, carry):
        @pl.when(q < NZ - AHEAD)
        def ahead():
            forward(q + AHEAD)

        k = turn(q)
        for s in range(1, NX):
            remote(shard(came_x(s), came_z(k)), shard(came_x(s), came_z(k)), gx_send.at[k, s], gx_recv.at[k, s],
                   at_x(s)).wait_recv()

        points = jnp.concatenate([xv[shard_rows(came_x(s), came_z(k)), 0:128] for s in range(NX)], axis=0)
        points = jnp.concatenate([points, sel[0 : NX * 128, :]], axis=1)
        top = total = None
        for j in range(m // TJ):
            s = dot(ya[j * TJ : (j + 1) * TJ, :], points, NT).reshape(TJ // 8, 8, NX * 128)
            here = jnp.max(s, axis=0)
            if j == 0:
                top = here
                total = jnp.sum(jnp.exp(s - top[None]), axis=0)
            else:
                upper = jnp.maximum(top, here)
                total = total * jnp.exp(top - upper) + jnp.sum(jnp.exp(s - upper[None]), axis=0)
                top = upper
        best = jnp.max(top, axis=0, keepdims=True)
        whole = jnp.sum(total * jnp.exp(top - best), axis=0, keepdims=True)
        for start, value in ((0, best), (nb, whole)):
            for s in range(NX):
                rowstat[pl.ds(start + came_x(s) * NZ + came_z(k), 1), :] = value[:, s * 128 : (s + 1) * 128]
        return carry

    for q in range(1, AHEAD):
        forward(q)
    lax.fori_loop(0, NZ, pass_1, 0)

    def spread(buf, send, recv, at, me, count):
        for k in range(1, count):
            remote(buf.at[me], buf.at[me], send.at[k], recv.at[k], at(k)).start()

    def collect(buf, send, recv, at, me, count):
        for k in range(1, count):
            remote(buf.at[me], buf.at[me], send.at[k], recv.at[k], at(k)).wait()

    def on_x(buf, slot):
        return (buf, x_send.at[slot], x_recv.at[slot], at_x, px, NX)

    def on_z(buf, slot):
        return (buf, z_send.at[slot], z_recv.at[slot], at_z, pz, NZ)

    def on_r(buf, slot):
        return (buf, r_send.at[slot], r_recv.at[slot], at_r, row, NR)

    def join(buf, count, size):
        tops = [buf[k, 0:size, :].astype(F32) for k in range(count)]
        sums = [buf[k, size : 2 * size, :].astype(F32) for k in range(count)]
        top = functools.reduce(jnp.maximum, tops)
        total = functools.reduce(lambda a, b: a + b, [s * jnp.exp(t - top) for t, s in zip(tops, sums)])
        return top, total

    def add(buf, count, size):
        return functools.reduce(lambda a, b: a + b, [buf[k, 0:size, :].astype(F32) for k in range(count)])

    def pack(ref, top, total):
        size = top.shape[0]
        near = top.astype(BF16)
        ref[0:size, :] = near
        ref[size : 2 * size, :] = (total * jnp.exp(top - near.astype(F32))).astype(BF16)

    def row_norms():
        def one(k, carry):
            norm = square_sums(xv[pl.ds(pl.multiple_of(k * TI, TI), TI), 0:128])
            xn[pl.ds(2 * k, 1), :] = norm[:, 0:128]
            xn[pl.ds(2 * k + 1, 1), :] = norm[:, 128:256]
            return carry

        lax.fori_loop(0, tiles, one, 0)

    pack(xpair.at[px], rowstat[0:nb, :], rowstat[nb : 2 * nb, :])
    spread(*on_x(xpair, 0))
    row_norms()
    collect(*on_x(xpair, 0))
    pack(zpair.at[pz], *join(xpair, NX, nb))
    spread(*on_z(zpair, 0))
    collect(*on_z(zpair, 0))
    top, total = join(zpair, NZ, nb)
    v1[...] = la_ref[...] - (top + jnp.log(total))
    alpha[...] = stack_pieces(flat(v1, nb), 3)

    def place(k, carry):
        cut = pl.ds(pl.multiple_of(k * TI, TI), TI)
        xv[cut, 128:144] = columns_of(alpha[:, cut], eye[...])
        return carry

    lax.fori_loop(0, tiles, place, 0, unroll=8)

    halves = range(2)
    nh, mh = n // 2, m // 2

    def block(q, carry):
        lanes = pl.ds(pl.multiple_of(q * WIDE, WIDE), WIDE)
        weights = jnp.concatenate([ya[lanes, 0:128], sel[...]], axis=1)
        top = None
        for t in range(tiles):
            s = dot(xv[t * TI : (t + 1) * TI, :], weights, NT)
            held[t * TI : (t + 1) * TI, :] = s
            here = jnp.max(s.reshape(TI // 8, 8, WIDE), axis=0)
            top = here if top is None else jnp.maximum(top, here)
        top = jnp.max(top, axis=0, keepdims=True)
        total = jnp.zeros((8, WIDE), F32)
        for t in range(tiles):
            e = jnp.exp(held[t * TI : (t + 1) * TI, :].reshape(TI // 8, 8, WIDE) - top[None])
            total = total + jnp.sum(e, axis=0)
            p[t * TI : (t + 1) * TI, lanes] = e.reshape(TI, WIDE).astype(BF16)
        best_col[:, lanes] = top
        sum_col[:, lanes] = jnp.sum(total, axis=0, keepdims=True)
        return carry

    def columns(c, count):
        lanes, rows = m // count, mb // count
        return slice(c * lanes, (c + 1) * lanes), slice(c * rows, (c + 1) * rows), rows

    for c in range(QUARTERS):
        lanes, _, size = columns(c, QUARTERS)
        lax.fori_loop(c * (m // QUARTERS // WIDE), (c + 1) * (m // QUARTERS // WIDE), block, 0)
        put(rpair.at[c, row], best_col[:, lanes])
        put(rpair.at[c, row], sum_col[:, lanes], size)
        spread(*on_r(rpair.at[c], c))

    def row_half(h):
        return slice(h * nh, (h + 1) * nh), slice(h * (nb // 2), (h + 1) * (nb // 2))

    def scale_of(step, c):
        count = QUARTERS if step == 1 else 2
        lanes, rows, size = columns(c, count)
        if step == 1:
            collect(*on_r(rpair.at[c], c))
            top, total = join(rpair.at[c], NR, size)
            lse[rows, :] = top + jnp.log(total)
            w[:, lanes] = jnp.exp(best_col[:, lanes] - flat(lse, size, c * size))
            return jnp.exp(lb_ref[:, lanes]) * w[:, lanes]
        collect(*on_r(rbuf.at[0, c], QUARTERS + c))
        colstat[rows, :] = add(rbuf.at[0, c], NR, size)
        return jnp.exp(lb_ref[:, lanes]) * w[:, lanes] / flat(colstat, size, c * size)

    for step in (1, 2):
        count = QUARTERS if step == 1 else 2
        for c in range(count):
            lanes = columns(c, count)[0]
            beta = stack_pieces(scale_of(step, c), 2)
            if c == 0:
                rowpart[...] = dot(beta, p[:, lanes], NT)[0:8, :]
            elif c < count - 1:
                rowpart[...] = rowpart[...] + dot(beta, p[:, lanes], NT)[0:8, :]
            else:
                for h in halves:
                    cut, rows = row_half(h)
                    both = rowpart[:, cut] + dot(beta, p[cut, lanes], NT)[0:8, :]
                    put(rowstat, jnp.sum(both, axis=0, keepdims=True), h * (nb // 2))
                    xbuf[step - 1, h, px] = rowstat[rows, :].astype(BF16)
                    spread(*on_x(xbuf.at[step - 1, h], 2 * step + h))
        for h in halves:
            collect(*on_x(xbuf.at[step - 1, h], 2 * step + h))
            zbuf[step - 1, h, pz] = add(xbuf.at[step - 1, h], NX, nb // 2).astype(BF16)
            spread(*on_z(zbuf.at[step - 1, h], 2 * step + h))
        for h in halves:
            cut, rows = row_half(h)
            collect(*on_z(zbuf.at[step - 1, h], 2 * step + h))
            rowsum = add(zbuf.at[step - 1, h], NZ, nb // 2)
            rowstat[rows, :] = jnp.exp(la_ref[rows, :]) / rowsum
            if step == 2:
                f_out[rows, :] = xn[rows, :] + 0.5 * (v1[rows, :] - jnp.log(rowsum))
            share = stack_pieces(flat(rowstat, nb // 2, h * (nb // 2)), 2)
            if h == 0:
                colpart[...] = dot(share, p[cut, :])[0:8, :]
            else:
                for c in halves:
                    lanes = columns(c, 2)[0]
                    both = colpart[:, lanes] + dot(share, p[cut, lanes])[0:8, :]
                    put(rbuf.at[step - 1, c, row], jnp.sum(both, axis=0, keepdims=True) * w[:, lanes])
                    spread(*on_r(rbuf.at[step - 1, c], QUARTERS + 2 * (step - 1) + c))
    for c in halves:
        rows = columns(c, 2)[1]
        collect(*on_r(rbuf.at[1, c], QUARTERS + 2 + c))
        g_out[rows, :] = yn[rows, :] - 0.5 * (lse[rows, :] + jnp.log(add(rbuf.at[1, c], NR, mb // 2)))

    for k in range(NZ):
        if k:
            z_copy(k).wait_send()
        for s in range(1, NX):
            x_copy(k, s).wait_send()


def local(logged, targets, log_a, log_b, start_g):
    n, m = log_a.shape[0], log_b.shape[0]
    nb, mb = n // 128, m // 128
    tiles = n // TI
    dma = pltpu.SemaphoreType.DMA
    vmem = pl.BlockSpec(memory_space=pltpu.VMEM)
    anywhere = pl.BlockSpec(memory_space=pltpu.HBM)
    f, g = pl.pallas_call(
        kernel,
        out_shape=(jax.ShapeDtypeStruct((nb, 128), F32), jax.ShapeDtypeStruct((mb, 128), F32)),
        in_specs=[anywhere] * 5,
        out_specs=(vmem, vmem),
        scratch_shapes=[
            pltpu.VMEM((m, 128), BF16),
            pltpu.VMEM((nb, 128), F32),
            pltpu.VMEM((1, m), F32),
            pltpu.VMEM((1, m), F32),
            pltpu.VMEM((n, 256), BF16),
            pltpu.VMEM((m, 256), BF16),
            pltpu.VMEM((n, m), BF16),
            pltpu.VMEM((n, WIDE), F32),
            pltpu.VMEM((TI, TI), BF16),
            pltpu.VMEM((WIDE, 128), BF16),
            pltpu.VMEM((1, m), F32),
            pltpu.VMEM((1, m), F32),
            pltpu.VMEM((1, m), F32),
            pltpu.VMEM((16, n), BF16),
            pltpu.VMEM((8, n), F32),
            pltpu.VMEM((8, m), F32),
            pltpu.VMEM((2 * nb, 128), F32),
            pltpu.VMEM((mb, 128), F32),
            pltpu.VMEM((nb, 128), F32),
            pltpu.VMEM((mb, 128), F32),
            pltpu.VMEM((nb, 128), F32),
            pltpu.VMEM((mb, 128), F32),
            pltpu.VMEM((NX, 2 * nb, 128), BF16),
            pltpu.VMEM((NZ, 2 * nb, 128), BF16),
            pltpu.VMEM((QUARTERS, NR, 2 * mb // QUARTERS, 128), F32),
            pltpu.VMEM((2, 2, NX, nb // 2, 128), BF16),
            pltpu.VMEM((2, 2, NZ, nb // 2, 128), BF16),
            pltpu.VMEM((2, 2, NR, mb // 2, 128), F32),
            dma((5,)),
            dma((NZ, NX)),
            dma((NZ, NX)),
            dma((NZ,)),
            dma((NZ,)),
            dma((6, NX)),
            dma((6, NX)),
            dma((6, NZ)),
            dma((6, NZ)),
            dma((QUARTERS + 4, NR)),
            dma((QUARTERS + 4, NR)),
        ],
        compiler_params=pltpu.CompilerParams(
            collective_id=0, has_side_effects=True, vmem_limit_bytes=64 * 1024 * 1024
        ),
    )(logged, targets, log_a.reshape(nb, 128), log_b.reshape(1, m), start_g.reshape(1, m))
    return f.reshape(n), g.reshape(m)


def solution(mesh):
    placed = (P(("rows", "cols"), None), P("cols", None), P("rows"), P("cols"), P("cols"))
    return jax.shard_map(
        local, mesh=mesh, in_specs=placed, out_specs=(P("rows"), P("cols")), check_vma=False
    )
```

```python
import functools

import jax
import jax.numpy as jnp
from jax import lax
from jax.experimental import pallas as pl
from jax.experimental.pallas import tpu as pltpu
from jax.sharding import PartitionSpec as P

NX, NZ, NR = 4, 8, 8
F32, BF16 = jnp.float32, jnp.bfloat16
AHEAD = 4
NT = (((1,), (1,)), ((), ()))
TI = 256
TJ = 256
WIDE = 512
QUARTERS = 4
MESH = pl.DeviceIdType.MESH


def dot(a, b, dims=(((1,), (0,)), ((), ()))):
    return lax.dot_general(a, b, dims, preferred_element_type=F32)


def flat(ref, rows, start=0):
    return jnp.concatenate([ref[start + k : start + k + 1, :] for k in range(rows)], axis=1)


def put(ref, value, start=0):
    for k in range(value.shape[1] // 128):
        ref[start + k : start + k + 1, :] = value[:, k * 128 : (k + 1) * 128]


def pieces(value, count):
    out = []
    for k in range(count):
        part = value.astype(BF16).astype(F32)
        out.append(part)
        value = value - part
    return out


def stack_pieces(value, count, rows=16):
    n = value.shape[1]
    index = lax.broadcasted_iota(jnp.int32, (rows, n), 0)
    out = jnp.zeros((rows, n), F32)
    for k, part in enumerate(pieces(value, count)):
        out = jnp.where(index == k, jnp.broadcast_to(part, (rows, n)), out)
    return out.astype(BF16)


def selector(rows, count):
    return (lax.broadcasted_iota(jnp.int32, (rows, 128), 1) < count).astype(F32).astype(BF16)


def square_sums(block):
    wide = block.astype(F32)
    high, low = pieces(wide * wide, 2)
    ones = jnp.ones((8, block.shape[1]), BF16)
    total = dot(ones, high.astype(BF16), NT) + dot(ones, low.astype(BF16), NT)
    return total[0:1, :]


def columns_of(stacked, eye):
    return dot(eye, stacked, NT).astype(BF16)


def kernel(
    x_hbm, y_hbm, la_hbm, lb_hbm, g_hbm, f_out, g_out,
    y_ref, la_ref, lb_ref, g_ref,
    xv, ya, p, held, eye, sel, best_col, sum_col, w, alpha, rowpart, colpart, rowstat, colstat, xn, yn, v1, lse,
    xpair, zpair, rpair, xbuf, zbuf, rbuf, local_sem,
    gx_send, gx_recv, gz_send, gz_recv, x_send, x_recv, z_send, z_recv, r_send, r_recv,
):
    n, m = xv.shape[0], ya.shape[0]
    nb, mb = n // 128, m // 128
    tiles = n // TI
    row = lax.axis_index("rows")
    col = lax.axis_index("cols")
    px, pz = col // NZ, lax.rem(col, NZ)

    def at_x(k):
        return (row, lax.rem(px + k, NX) * NZ + pz)

    def at_z(k):
        return (row, px * NZ + lax.rem(pz + k, NZ))

    def at_r(k):
        return (lax.rem(row + k, NR), col)

    barrier = pltpu.get_barrier_semaphore()
    for at, count in ((at_x, NX), (at_z, NZ), (at_r, NR)):
        for k in range(1, count):
            pl.semaphore_signal(barrier, inc=1, device_id=at(k), device_id_type=MESH)

    own_rows = pl.ds(pl.multiple_of(col * 128, 128), 128)
    moves = (
        (x_hbm, xv.at[own_rows, pl.ds(0, 128)]), (y_hbm, y_ref), (la_hbm, la_ref), (lb_hbm, lb_ref), (g_hbm, g_ref),
    )
    fetch = [pltpu.make_async_copy(src, dst, local_sem.at[k]) for k, (src, dst) in enumerate(moves)]
    for one in fetch:
        one.start()
    index = lax.broadcasted_iota(jnp.int32, (TI, TI), 0) == lax.broadcasted_iota(jnp.int32, (TI, TI), 1)
    eye[...] = jnp.where(index, 1.0, 0.0).astype(BF16)
    sel[...] = selector(sel.shape[0], 3)
    ya[:, 128:256] = jnp.zeros((m, 128), BF16)
    xv[:, 128:256] = jnp.zeros((n, 128), BF16)
    fetch[0].wait()
    pl.semaphore_wait(barrier, NX + NZ + NR - 3)

    def remote(src, dst, send, recv, device):
        return pltpu.make_async_remote_copy(
            src_ref=src, dst_ref=dst, send_sem=send, recv_sem=recv, device_id=device, device_id_type=MESH
        )

    def came_x(s):
        return lax.rem(px + NX - s, NX)

    def came_z(k):
        return lax.rem(pz + NZ - k, NZ)

    def shard_rows(cx, cz):
        return pl.ds(pl.multiple_of((cx * NZ + cz) * 128, 128), 128)

    def shard(cx, cz):
        return xv.at[shard_rows(cx, cz), pl.ds(0, 128)]

    def z_copy(k):
        own = shard(px, pz)
        return remote(own, own, gz_send, gz_recv.at[k], at_z(k))

    def x_copy(k, s):
        block = shard(px, came_z(k))
        return remote(block, block, gx_send, gx_recv.at[k], at_x(s))

    def shards(count):
        return xv.at[pl.ds(0, count * 128), pl.ds(0, 128)]

    def turn(q):
        odd = lax.rem(q, 2)
        return odd * ((q + 1) // 2) + (1 - odd) * lax.rem(NZ - q // 2, NZ)

    for s in (1, 3, 2):
        x_copy(0, s).start()
    for q in range(1, NZ):
        z_copy((q + 1) // 2 if q % 2 else NZ - q // 2).start()
    for one in fetch[1:]:
        one.wait()

    for k in range(m // TI):
        cut = pl.ds(k * TI, TI)
        block = y_ref[cut, :]
        ya[cut, 0:128] = (block.astype(F32) * 4.0).astype(BF16)
        norm = square_sums(block)
        put(yn, norm, 2 * k)
        u = lb_ref[:, cut] + 2.0 * g_ref[:, cut] - 2.0 * norm
        ya[cut, 128:144] = columns_of(stack_pieces(u, 3), eye[...])

    def forward(q):
        k = turn(q)
        z_copy(k).wait_recv()
        for s in (1, 3, 2):
            x_copy(k, s).start()

    def pass_1(q, carry):
        @pl.when(q < NZ - AHEAD)
        def ahead():
            forward(q + AHEAD)

        k = turn(q)
        remote(shards(NX - 1), shards(NX - 1), gx_send, gx_recv.at[k], at_x(1)).wait_recv()
        points = jnp.concatenate([xv[shard_rows(came_x(s), came_z(k)), 0:128] for s in range(NX)], axis=0)
        points = jnp.concatenate([points, sel[0 : NX * 128, :]], axis=1)
        top = total = None
        for j in range(m // TJ):
            s = dot(ya[j * TJ : (j + 1) * TJ, :], points, NT).reshape(TJ // 8, 8, NX * 128)
            here = jnp.max(s, axis=0)
            if j == 0:
                top = here
                total = jnp.sum(jnp.exp(s - top[None]), axis=0)
            else:
                upper = jnp.maximum(top, here)
                total = total * jnp.exp(top - upper) + jnp.sum(jnp.exp(s - upper[None]), axis=0)
                top = upper
        best = jnp.max(top, axis=0, keepdims=True)
        whole = jnp.sum(total * jnp.exp(top - best), axis=0, keepdims=True)
        for start, value in ((0, best), (nb, whole)):
            for s in range(NX):
                rowstat[pl.ds(start + came_x(s) * NZ + came_z(k), 1), :] = value[:, s * 128 : (s + 1) * 128]
        return carry

    for q in range(1, AHEAD):
        forward(q)
    lax.fori_loop(0, NZ, pass_1, 0)

    def spread(buf, send, recv, at, me, count):
        for k in range(1, count):
            remote(buf.at[me], buf.at[me], send, recv, at(k)).start()

    def collect(buf, send, recv, at, me, count):
        others = buf.at[pl.ds(0, count - 1)]
        remote(others, others, send, recv, at(1)).wait()

    def on_x(buf, slot):
        return (buf, x_send.at[slot], x_recv.at[slot], at_x, px, NX)

    def on_z(buf, slot):
        return (buf, z_send.at[slot], z_recv.at[slot], at_z, pz, NZ)

    def on_r(buf, slot):
        return (buf, r_send.at[slot], r_recv.at[slot], at_r, row, NR)

    def join(buf, count, size):
        tops = [buf[k, 0:size, :].astype(F32) for k in range(count)]
        sums = [buf[k, size : 2 * size, :].astype(F32) for k in range(count)]
        top = functools.reduce(jnp.maximum, tops)
        total = functools.reduce(lambda a, b: a + b, [s * jnp.exp(t - top) for t, s in zip(tops, sums)])
        return top, total

    def add(buf, count, size):
        return functools.reduce(lambda a, b: a + b, [buf[k, 0:size, :].astype(F32) for k in range(count)])

    def pack(ref, top, total):
        size = top.shape[0]
        near = top.astype(BF16)
        ref[0:size, :] = near
        ref[size : 2 * size, :] = (total * jnp.exp(top - near.astype(F32))).astype(BF16)

    def row_norms():
        def one(k, carry):
            norm = square_sums(xv[pl.ds(pl.multiple_of(k * TI, TI), TI), 0:128])
            xn[pl.ds(2 * k, 1), :] = norm[:, 0:128]
            xn[pl.ds(2 * k + 1, 1), :] = norm[:, 128:256]
            return carry

        lax.fori_loop(0, tiles, one, 0)

    pack(xpair.at[px], rowstat[0:nb, :], rowstat[nb : 2 * nb, :])
    spread(*on_x(xpair, 0))
    row_norms()
    collect(*on_x(xpair, 0))
    pack(zpair.at[pz], *join(xpair, NX, nb))
    spread(*on_z(zpair, 0))
    collect(*on_z(zpair, 0))
    top, total = join(zpair, NZ, nb)
    v1[...] = la_ref[...] - (top + jnp.log(total))
    alpha[...] = stack_pieces(flat(v1, nb), 3)

    def place(k, carry):
        cut = pl.ds(pl.multiple_of(k * TI, TI), TI)
        xv[cut, 128:144] = columns_of(alpha[:, cut], eye[...])
        return carry

    lax.fori_loop(0, tiles, place, 0, unroll=8)

    halves = range(2)
    nh, mh = n // 2, m // 2

    def block(q, carry):
        lanes = pl.ds(pl.multiple_of(q * WIDE, WIDE), WIDE)
        weights = jnp.concatenate([ya[lanes, 0:128], sel[...]], axis=1)
        top = None
        for t in range(tiles):
            s = dot(xv[t * TI : (t + 1) * TI, :], weights, NT)
            held[t * TI : (t + 1) * TI, :] = s
            here = jnp.max(s.reshape(TI // 8, 8, WIDE), axis=0)
            top = here if top is None else jnp.maximum(top, here)
        top = jnp.max(top, axis=0, keepdims=True)
        total = jnp.zeros((8, WIDE), F32)
        for t in range(tiles):
            e = jnp.exp(held[t * TI : (t + 1) * TI, :].reshape(TI // 8, 8, WIDE) - top[None])
            total = total + jnp.sum(e, axis=0)
            p[t * TI : (t + 1) * TI, lanes] = e.reshape(TI, WIDE).astype(BF16)
        best_col[:, lanes] = top
        sum_col[:, lanes] = jnp.sum(total, axis=0, keepdims=True)
        return carry

    def columns(c, count):
        lanes, rows = m // count, mb // count
        return slice(c * lanes, (c + 1) * lanes), slice(c * rows, (c + 1) * rows), rows

    for c in range(QUARTERS):
        lanes, _, size = columns(c, QUARTERS)
        lax.fori_loop(c * (m // QUARTERS // WIDE), (c + 1) * (m // QUARTERS // WIDE), block, 0)
        put(rpair.at[c, row], best_col[:, lanes])
        put(rpair.at[c, row], sum_col[:, lanes], size)
        spread(*on_r(rpair.at[c], c))

    def row_half(h):
        return slice(h * nh, (h + 1) * nh), slice(h * (nb // 2), (h + 1) * (nb // 2))

    def scale_of(step, c):
        count = QUARTERS if step == 1 else 2
        lanes, rows, size = columns(c, count)
        if step == 1:
            collect(*on_r(rpair.at[c], c))
            top, total = join(rpair.at[c], NR, size)
            lse[rows, :] = top + jnp.log(total)
            w[:, lanes] = jnp.exp(best_col[:, lanes] - flat(lse, size, c * size))
            return jnp.exp(lb_ref[:, lanes]) * w[:, lanes]
        collect(*on_r(rbuf.at[0, c], QUARTERS + c))
        colstat[rows, :] = add(rbuf.at[0, c], NR, size)
        return jnp.exp(lb_ref[:, lanes]) * w[:, lanes] / flat(colstat, size, c * size)

    for step in (1, 2):
        count = QUARTERS if step == 1 else 2
        for c in range(count):
            lanes = columns(c, count)[0]
            beta = stack_pieces(scale_of(step, c), 2)
            if c == 0:
                rowpart[...] = dot(beta, p[:, lanes], NT)[0:8, :]
            elif c < count - 1:
                rowpart[...] = rowpart[...] + dot(beta, p[:, lanes], NT)[0:8, :]
            else:
                for h in halves:
                    cut, rows = row_half(h)
                    both = rowpart[:, cut] + dot(beta, p[cut, lanes], NT)[0:8, :]
                    put(rowstat, jnp.sum(both, axis=0, keepdims=True), h * (nb // 2))
                    xbuf[step - 1, h, px] = rowstat[rows, :].astype(BF16)
                    spread(*on_x(xbuf.at[step - 1, h], 2 * step + h))
        for h in halves:
            collect(*on_x(xbuf.at[step - 1, h], 2 * step + h))
            zbuf[step - 1, h, pz] = add(xbuf.at[step - 1, h], NX, nb // 2).astype(BF16)
            spread(*on_z(zbuf.at[step - 1, h], 2 * step + h))
        for h in halves:
            cut, rows = row_half(h)
            collect(*on_z(zbuf.at[step - 1, h], 2 * step + h))
            rowsum = add(zbuf.at[step - 1, h], NZ, nb // 2)
            rowstat[rows, :] = jnp.exp(la_ref[rows, :]) / rowsum
            if step == 2:
                f_out[rows, :] = xn[rows, :] + 0.5 * (v1[rows, :] - jnp.log(rowsum))
            share = stack_pieces(flat(rowstat, nb // 2, h * (nb // 2)), 2)
            if h == 0:
                colpart[...] = dot(share, p[cut, :])[0:8, :]
            else:
                for c in halves:
                    lanes = columns(c, 2)[0]
                    both = colpart[:, lanes] + dot(share, p[cut, lanes])[0:8, :]
                    put(rbuf.at[step - 1, c, row], jnp.sum(both, axis=0, keepdims=True) * w[:, lanes])
                    spread(*on_r(rbuf.at[step - 1, c], QUARTERS + 2 * (step - 1) + c))
    for c in halves:
        rows = columns(c, 2)[1]
        collect(*on_r(rbuf.at[1, c], QUARTERS + 2 + c))
        g_out[rows, :] = yn[rows, :] - 0.5 * (lse[rows, :] + jnp.log(add(rbuf.at[1, c], NR, mb // 2)))

    remote(shards(NZ - 1), shards(NZ - 1), gz_send, gz_recv.at[1], at_z(1)).wait_send()
    remote(shards(NZ * (NX - 1)), shards(NZ * (NX - 1)), gx_send, gx_recv.at[0], at_x(1)).wait_send()


def local(logged, targets, log_a, log_b, start_g):
    n, m = log_a.shape[0], log_b.shape[0]
    nb, mb = n // 128, m // 128
    tiles = n // TI
    dma = pltpu.SemaphoreType.DMA
    vmem = pl.BlockSpec(memory_space=pltpu.VMEM)
    anywhere = pl.BlockSpec(memory_space=pltpu.HBM)
    f, g = pl.pallas_call(
        kernel,
        out_shape=(jax.ShapeDtypeStruct((nb, 128), F32), jax.ShapeDtypeStruct((mb, 128), F32)),
        in_specs=[anywhere] * 5,
        out_specs=(vmem, vmem),
        scratch_shapes=[
            pltpu.VMEM((m, 128), BF16),
            pltpu.VMEM((nb, 128), F32),
            pltpu.VMEM((1, m), F32),
            pltpu.VMEM((1, m), F32),
            pltpu.VMEM((n, 256), BF16),
            pltpu.VMEM((m, 256), BF16),
            pltpu.VMEM((n, m), BF16),
            pltpu.VMEM((n, WIDE), F32),
            pltpu.VMEM((TI, TI), BF16),
            pltpu.VMEM((WIDE, 128), BF16),
            pltpu.VMEM((1, m), F32),
            pltpu.VMEM((1, m), F32),
            pltpu.VMEM((1, m), F32),
            pltpu.VMEM((16, n), BF16),
            pltpu.VMEM((8, n), F32),
            pltpu.VMEM((8, m), F32),
            pltpu.VMEM((2 * nb, 128), F32),
            pltpu.VMEM((mb, 128), F32),
            pltpu.VMEM((nb, 128), F32),
            pltpu.VMEM((mb, 128), F32),
            pltpu.VMEM((nb, 128), F32),
            pltpu.VMEM((mb, 128), F32),
            pltpu.VMEM((NX, 2 * nb, 128), BF16),
            pltpu.VMEM((NZ, 2 * nb, 128), BF16),
            pltpu.VMEM((QUARTERS, NR, 2 * mb // QUARTERS, 128), F32),
            pltpu.VMEM((2, 2, NX, nb // 2, 128), BF16),
            pltpu.VMEM((2, 2, NZ, nb // 2, 128), BF16),
            pltpu.VMEM((2, 2, NR, mb // 2, 128), F32),
            dma((5,)),
            dma(()),
            dma((NZ,)),
            dma(()),
            dma((NZ,)),
            dma((6,)),
            dma((6,)),
            dma((6,)),
            dma((6,)),
            dma((QUARTERS + 4,)),
            dma((QUARTERS + 4,)),
        ],
        compiler_params=pltpu.CompilerParams(
            collective_id=0, has_side_effects=True, vmem_limit_bytes=64 * 1024 * 1024
        ),
    )(logged, targets, log_a.reshape(nb, 128), log_b.reshape(1, m), start_g.reshape(1, m))
    return f.reshape(n), g.reshape(m)


def solution(mesh):
    placed = (P(("rows", "cols"), None), P("cols", None), P("rows"), P("cols"), P("cols"))
    return jax.shard_map(
        local, mesh=mesh, in_specs=placed, out_specs=(P("rows"), P("cols")), check_vma=False
    )
```

```python
import functools

import jax
import jax.numpy as jnp
from jax import lax
from jax.experimental import pallas as pl
from jax.experimental.pallas import tpu as pltpu
from jax.sharding import PartitionSpec as P

NX, NZ, NR = 4, 8, 8
F32, BF16 = jnp.float32, jnp.bfloat16
AHEAD = 4
NT = (((1,), (1,)), ((), ()))
TI = 256
TJ = 256
WIDE = 512
QUARTERS = 4
MESH = pl.DeviceIdType.MESH


def dot(a, b, dims=(((1,), (0,)), ((), ()))):
    return lax.dot_general(a, b, dims, preferred_element_type=F32)


def flat(ref, rows, start=0):
    return jnp.concatenate([ref[start + k : start + k + 1, :] for k in range(rows)], axis=1)


def put(ref, value, start=0):
    for k in range(value.shape[1] // 128):
        ref[start + k : start + k + 1, :] = value[:, k * 128 : (k + 1) * 128]


def pieces(value, count):
    out = []
    for k in range(count):
        part = value.astype(BF16).astype(F32)
        out.append(part)
        value = value - part
    return out


def stack_pieces(value, count, rows=16):
    n = value.shape[1]
    index = lax.broadcasted_iota(jnp.int32, (rows, n), 0)
    out = jnp.zeros((rows, n), F32)
    for k, part in enumerate(pieces(value, count)):
        out = jnp.where(index == k, jnp.broadcast_to(part, (rows, n)), out)
    return out.astype(BF16)


def selector(rows, count):
    return (lax.broadcasted_iota(jnp.int32, (rows, 128), 1) < count).astype(F32).astype(BF16)


def square_sums(block):
    wide = block.astype(F32)
    high, low = pieces(wide * wide, 2)
    ones = jnp.ones((8, block.shape[1]), BF16)
    total = dot(ones, high.astype(BF16), NT) + dot(ones, low.astype(BF16), NT)
    return total[0:1, :]


def columns_of(stacked, eye):
    return dot(eye, stacked, NT).astype(BF16)


def kernel(
    x_hbm, y_hbm, la_hbm, lb_hbm, g_hbm, f_out, g_out,
    y_ref, la_ref, lb_ref, g_ref,
    xv, ya, p, held, eye, sel, best_col, sum_col, w, alpha, rowpart, colpart, rowstat, colstat, xn, yn, v1, lse,
    xpair, zpair, rpair, xbuf, zbuf, rbuf, local_sem,
    gx_send, gx_recv, gz_send, gz_recv, x_send, x_recv, z_send, z_recv, r_send, r_recv,
):
    n, m = xv.shape[0], ya.shape[0]
    nb, mb = n // 128, m // 128
    tiles = n // TI
    row = lax.axis_index("rows")
    col = lax.axis_index("cols")
    px, pz = col // NZ, lax.rem(col, NZ)

    def at_x(k):
        return (row, lax.rem(px + k, NX) * NZ + pz)

    def at_z(k):
        return (row, px * NZ + lax.rem(pz + k, NZ))

    def at_r(k):
        return (lax.rem(row + k, NR), col)

    barrier = pltpu.get_barrier_semaphore()
    for at, count in ((at_x, NX), (at_z, NZ), (at_r, NR)):
        for k in range(1, count):
            pl.semaphore_signal(barrier, inc=1, device_id=at(k), device_id_type=MESH)

    own_rows = pl.ds(pl.multiple_of(col * 128, 128), 128)
    moves = (
        (x_hbm, xv.at[own_rows, pl.ds(0, 128)]), (y_hbm, y_ref), (la_hbm, la_ref), (lb_hbm, lb_ref), (g_hbm, g_ref),
    )
    fetch = [pltpu.make_async_copy(src, dst, local_sem.at[k]) for k, (src, dst) in enumerate(moves)]
    for one in fetch:
        one.start()
    index = lax.broadcasted_iota(jnp.int32, (TI, TI), 0) == lax.broadcasted_iota(jnp.int32, (TI, TI), 1)
    eye[...] = jnp.where(index, 1.0, 0.0).astype(BF16)
    sel[...] = selector(sel.shape[0], 3)
    ya[:, 128:256] = jnp.zeros((m, 128), BF16)
    xv[:, 128:256] = jnp.zeros((n, 128), BF16)
    fetch[0].wait()
    pl.semaphore_wait(barrier, NX + NZ + NR - 3)

    def remote(src, dst, send, recv, device):
        return pltpu.make_async_remote_copy(
            src_ref=src, dst_ref=dst, send_sem=send, recv_sem=recv, device_id=device, device_id_type=MESH
        )

    def came_x(s):
        return lax.rem(px + NX - s, NX)

    def came_z(k):
        return lax.rem(pz + NZ - k, NZ)

    def shard_rows(cx, cz):
        return pl.ds(pl.multiple_of((cx * NZ + cz) * 128, 128), 128)

    def shard(cx, cz):
        return xv.at[shard_rows(cx, cz), pl.ds(0, 128)]

    def z_copy(k):
        own = shard(px, pz)
        return remote(own, own, gz_send, gz_recv.at[k], at_z(k))

    def x_copy(k, s):
        block = shard(px, came_z(k))
        return remote(block, block, gx_send, gx_recv.at[k], at_x(s))

    def shards(count):
        return xv.at[pl.ds(0, count * 128), pl.ds(0, 128)]

    def turn(q):
        odd = lax.rem(q, 2)
        return odd * ((q + 1) // 2) + (1 - odd) * lax.rem(NZ - q // 2, NZ)

    for s in (1, 3, 2):
        x_copy(0, s).start()
    for q in range(1, NZ):
        z_copy((q + 1) // 2 if q % 2 else NZ - q // 2).start()
    for one in fetch[1:]:
        one.wait()

    for k in range(m // TI):
        cut = pl.ds(k * TI, TI)
        block = y_ref[cut, :]
        ya[cut, 0:128] = (block.astype(F32) * 4.0).astype(BF16)
        norm = square_sums(block)
        put(yn, norm, 2 * k)
        u = lb_ref[:, cut] + 2.0 * g_ref[:, cut] - 2.0 * norm
        ya[cut, 128:144] = columns_of(stack_pieces(u, 3), eye[...])

    def forward(q):
        k = turn(q)
        z_copy(k).wait_recv()
        for s in (1, 3, 2):
            x_copy(k, s).start()

    def pass_1(q, carry):
        @pl.when(q < NZ - AHEAD)
        def ahead():
            forward(q + AHEAD)

        k = turn(q)
        remote(shards(NX - 1), shards(NX - 1), gx_send, gx_recv.at[k], at_x(1)).wait_recv()
        points = jnp.concatenate([xv[shard_rows(came_x(s), came_z(k)), 0:128] for s in range(NX)], axis=0)
        points = jnp.concatenate([points, sel[0 : NX * 128, :]], axis=1)
        top = total = None
        for j in range(m // TJ):
            s = dot(ya[j * TJ : (j + 1) * TJ, :], points, NT).reshape(TJ // 8, 8, NX * 128)
            here = jnp.max(s, axis=0)
            if j == 0:
                top = here
                total = jnp.sum(jnp.exp(s - top[None]), axis=0)
            else:
                upper = jnp.maximum(top, here)
                total = total * jnp.exp(top - upper) + jnp.sum(jnp.exp(s - upper[None]), axis=0)
                top = upper
        best = jnp.max(top, axis=0, keepdims=True)
        whole = jnp.sum(total * jnp.exp(top - best), axis=0, keepdims=True)
        for start, value in ((0, best), (nb, whole)):
            for s in range(NX):
                rowstat[pl.ds(start + came_x(s) * NZ + came_z(k), 1), :] = value[:, s * 128 : (s + 1) * 128]
        return carry

    for q in range(1, AHEAD):
        forward(q)
    lax.fori_loop(0, NZ, pass_1, 0)

    def spread(buf, send, recv, at, me, count):
        for k in range(1, count):
            remote(buf.at[me], buf.at[me], send, recv, at(k)).start()

    def collect(buf, send, recv, at, me, count):
        others = buf.at[pl.ds(0, count - 1)]
        remote(others, others, send, recv, at(1)).wait()

    def on_x(buf, slot):
        return (buf, x_send.at[slot], x_recv.at[slot], at_x, px, NX)

    def on_z(buf, slot):
        return (buf, z_send.at[slot], z_recv.at[slot], at_z, pz, NZ)

    def on_r(buf, slot):
        return (buf, r_send.at[slot], r_recv.at[slot], at_r, row, NR)

    def join(buf, count, size):
        tops = [buf[k, 0:size, :].astype(F32) for k in range(count)]
        sums = [buf[k, size : 2 * size, :].astype(F32) for k in range(count)]
        top = functools.reduce(jnp.maximum, tops)
        total = functools.reduce(lambda a, b: a + b, [s * jnp.exp(t - top) for t, s in zip(tops, sums)])
        return top, total

    def add(buf, count, size):
        return functools.reduce(lambda a, b: a + b, [buf[k, 0:size, :].astype(F32) for k in range(count)])

    def pack(ref, top, total):
        size = top.shape[0]
        near = top.astype(BF16)
        ref[0:size, :] = near
        ref[size : 2 * size, :] = (total * jnp.exp(top - near.astype(F32))).astype(BF16)

    def row_norms():
        def one(k, carry):
            norm = square_sums(xv[pl.ds(pl.multiple_of(k * TI, TI), TI), 0:128])
            xn[pl.ds(2 * k, 1), :] = norm[:, 0:128]
            xn[pl.ds(2 * k + 1, 1), :] = norm[:, 128:256]
            return carry

        lax.fori_loop(0, tiles, one, 0, unroll=8)

    pack(xpair.at[px], rowstat[0:nb, :], rowstat[nb : 2 * nb, :])
    spread(*on_x(xpair, 0))
    row_norms()
    collect(*on_x(xpair, 0))
    pack(zpair.at[pz], *join(xpair, NX, nb))
    spread(*on_z(zpair, 0))
    collect(*on_z(zpair, 0))
    top, total = join(zpair, NZ, nb)
    v1[...] = la_ref[...] - (top + jnp.log(total))
    alpha[...] = stack_pieces(flat(v1, nb), 3)

    def place(k, carry):
        cut = pl.ds(pl.multiple_of(k * TI, TI), TI)
        xv[cut, 128:144] = columns_of(alpha[:, cut], eye[...])
        return carry

    lax.fori_loop(0, tiles, place, 0, unroll=8)

    halves = range(2)
    nh, mh = n // 2, m // 2

    def block(q, carry):
        lanes = pl.ds(pl.multiple_of(q * WIDE, WIDE), WIDE)
        weights = jnp.concatenate([ya[lanes, 0:128], sel[...]], axis=1)
        top = None
        for t in range(tiles):
            s = dot(xv[t * TI : (t + 1) * TI, :], weights, NT)
            held[t * TI : (t + 1) * TI, :] = s
            here = jnp.max(s.reshape(TI // 8, 8, WIDE), axis=0)
            top = here if top is None else jnp.maximum(top, here)
        top = jnp.max(top, axis=0, keepdims=True)
        total = jnp.zeros((8, WIDE), F32)
        for t in range(tiles):
            e = jnp.exp(held[t * TI : (t + 1) * TI, :].reshape(TI // 8, 8, WIDE) - top[None])
            total = total + jnp.sum(e, axis=0)
            p[t * TI : (t + 1) * TI, lanes] = e.reshape(TI, WIDE).astype(BF16)
        best_col[:, lanes] = top
        sum_col[:, lanes] = jnp.sum(total, axis=0, keepdims=True)
        return carry

    def columns(c, count):
        lanes, rows = m // count, mb // count
        return slice(c * lanes, (c + 1) * lanes), slice(c * rows, (c + 1) * rows), rows

    for c in range(QUARTERS):
        lanes, _, size = columns(c, QUARTERS)
        lax.fori_loop(c * (m // QUARTERS // WIDE), (c + 1) * (m // QUARTERS // WIDE), block, 0)
        put(rpair.at[c, row], best_col[:, lanes])
        put(rpair.at[c, row], sum_col[:, lanes], size)
        spread(*on_r(rpair.at[c], c))

    def row_half(h):
        return slice(h * nh, (h + 1) * nh), slice(h * (nb // 2), (h + 1) * (nb // 2))

    def scale_of(step, c):
        count = QUARTERS if step == 1 else 2
        lanes, rows, size = columns(c, count)
        if step == 1:
            collect(*on_r(rpair.at[c], c))
            top, total = join(rpair.at[c], NR, size)
            lse[rows, :] = top + jnp.log(total)
            w[:, lanes] = jnp.exp(best_col[:, lanes] - flat(lse, size, c * size))
            return jnp.exp(lb_ref[:, lanes]) * w[:, lanes]
        collect(*on_r(rbuf.at[0, c], QUARTERS + c))
        colstat[rows, :] = add(rbuf.at[0, c], NR, size)
        return jnp.exp(lb_ref[:, lanes]) * w[:, lanes] / flat(colstat, size, c * size)

    for step in (1, 2):
        count = QUARTERS if step == 1 else 2
        for c in range(count):
            lanes = columns(c, count)[0]
            beta = stack_pieces(scale_of(step, c), 2)
            if c == 0:
                rowpart[...] = dot(beta, p[:, lanes], NT)[0:8, :]
            elif c < count - 1:
                rowpart[...] = rowpart[...] + dot(beta, p[:, lanes], NT)[0:8, :]
            else:
                for h in halves:
                    cut, rows = row_half(h)
                    both = rowpart[:, cut] + dot(beta, p[cut, lanes], NT)[0:8, :]
                    put(rowstat, jnp.sum(both, axis=0, keepdims=True), h * (nb // 2))
                    xbuf[step - 1, h, px] = rowstat[rows, :].astype(BF16)
                    spread(*on_x(xbuf.at[step - 1, h], 2 * step + h))
        for h in halves:
            collect(*on_x(xbuf.at[step - 1, h], 2 * step + h))
            zbuf[step - 1, h, pz] = add(xbuf.at[step - 1, h], NX, nb // 2).astype(BF16)
            spread(*on_z(zbuf.at[step - 1, h], 2 * step + h))
        for h in halves:
            cut, rows = row_half(h)
            collect(*on_z(zbuf.at[step - 1, h], 2 * step + h))
            rowsum = add(zbuf.at[step - 1, h], NZ, nb // 2)
            rowstat[rows, :] = jnp.exp(la_ref[rows, :]) / rowsum
            if step == 2:
                f_out[rows, :] = xn[rows, :] + 0.5 * (v1[rows, :] - jnp.log(rowsum))
            share = stack_pieces(flat(rowstat, nb // 2, h * (nb // 2)), 2)
            if h == 0:
                colpart[...] = dot(share, p[cut, :])[0:8, :]
            else:
                for c in halves:
                    lanes = columns(c, 2)[0]
                    both = colpart[:, lanes] + dot(share, p[cut, lanes])[0:8, :]
                    put(rbuf.at[step - 1, c, row], jnp.sum(both, axis=0, keepdims=True) * w[:, lanes])
                    spread(*on_r(rbuf.at[step - 1, c], QUARTERS + 2 * (step - 1) + c))
    for c in halves:
        rows = columns(c, 2)[1]
        collect(*on_r(rbuf.at[1, c], QUARTERS + 2 + c))
        g_out[rows, :] = yn[rows, :] - 0.5 * (lse[rows, :] + jnp.log(add(rbuf.at[1, c], NR, mb // 2)))

    remote(shards(NZ - 1), shards(NZ - 1), gz_send, gz_recv.at[1], at_z(1)).wait_send()
    remote(shards(NZ * (NX - 1)), shards(NZ * (NX - 1)), gx_send, gx_recv.at[0], at_x(1)).wait_send()


def local(logged, targets, log_a, log_b, start_g):
    n, m = log_a.shape[0], log_b.shape[0]
    nb, mb = n // 128, m // 128
    tiles = n // TI
    dma = pltpu.SemaphoreType.DMA
    vmem = pl.BlockSpec(memory_space=pltpu.VMEM)
    anywhere = pl.BlockSpec(memory_space=pltpu.HBM)
    f, g = pl.pallas_call(
        kernel,
        out_shape=(jax.ShapeDtypeStruct((nb, 128), F32), jax.ShapeDtypeStruct((mb, 128), F32)),
        in_specs=[anywhere] * 5,
        out_specs=(vmem, vmem),
        scratch_shapes=[
            pltpu.VMEM((m, 128), BF16),
            pltpu.VMEM((nb, 128), F32),
            pltpu.VMEM((1, m), F32),
            pltpu.VMEM((1, m), F32),
            pltpu.VMEM((n, 256), BF16),
            pltpu.VMEM((m, 256), BF16),
            pltpu.VMEM((n, m), BF16),
            pltpu.VMEM((n, WIDE), F32),
            pltpu.VMEM((TI, TI), BF16),
            pltpu.VMEM((WIDE, 128), BF16),
            pltpu.VMEM((1, m), F32),
            pltpu.VMEM((1, m), F32),
            pltpu.VMEM((1, m), F32),
            pltpu.VMEM((16, n), BF16),
            pltpu.VMEM((8, n), F32),
            pltpu.VMEM((8, m), F32),
            pltpu.VMEM((2 * nb, 128), F32),
            pltpu.VMEM((mb, 128), F32),
            pltpu.VMEM((nb, 128), F32),
            pltpu.VMEM((mb, 128), F32),
            pltpu.VMEM((nb, 128), F32),
            pltpu.VMEM((mb, 128), F32),
            pltpu.VMEM((NX, 2 * nb, 128), BF16),
            pltpu.VMEM((NZ, 2 * nb, 128), BF16),
            pltpu.VMEM((QUARTERS, NR, 2 * mb // QUARTERS, 128), F32),
            pltpu.VMEM((2, 2, NX, nb // 2, 128), BF16),
            pltpu.VMEM((2, 2, NZ, nb // 2, 128), BF16),
            pltpu.VMEM((2, 2, NR, mb // 2, 128), F32),
            dma((5,)),
            dma(()),
            dma((NZ,)),
            dma(()),
            dma((NZ,)),
            dma((6,)),
            dma((6,)),
            dma((6,)),
            dma((6,)),
            dma((QUARTERS + 4,)),
            dma((QUARTERS + 4,)),
        ],
        compiler_params=pltpu.CompilerParams(
            collective_id=0, has_side_effects=True, vmem_limit_bytes=64 * 1024 * 1024
        ),
    )(logged, targets, log_a.reshape(nb, 128), log_b.reshape(1, m), start_g.reshape(1, m))
    return f.reshape(n), g.reshape(m)


def solution(mesh):
    placed = (P(("rows", "cols"), None), P("cols", None), P("rows"), P("cols"), P("cols"))
    return jax.shard_map(
        local, mesh=mesh, in_specs=placed, out_specs=(P("rows"), P("cols")), check_vma=False
    )
```
